512 devices in a mesh: tile: 64 (over z, x, core), lev: 8 (over y).
Axes of the slice: x: 4, y: 8, z: 8, core: 2. Of those that a mesh axis runs over, the one named last changes fastest.
Arguments:
- tracers: bfloat16 [8, 32, 1024, 128], P(None, 'lev', 'tile'), may hold values from -6 to 6
- wind_field: bfloat16 [3, 32, 1024, 128], P(None, 'lev', 'tile'), may hold values from -5 to 5
- regions: int32 [4, 1024, 2], P(None, 'tile'), may hold values from 0 to 62, as said below
- stencil_base: int32 [4, 2, 1024, 128], P(None, None, 'tile'), may hold values from 0 to 28, as said below
- far_start: int32 [4, 64, 2], replicated, may hold values from 0 to 15, as said below
Outputs:
- tracers_new: bfloat16 [8, 32, 1024, 128], P(None, 'lev', 'tile')
- displacement: float32 [3, 32, 1024, 128], P(None, 'lev', 'tile')
The draws below stay inside these ranges and needn't reach their ends.
Inputs may be any that keep to these rules, and one draw needn't show every extreme that they name: For an arrival block of band r, regions[k, j, 0] lies in r - 2 to r + 1 and in 0 to 62, and regions[k, j, 1] in 0 to 15. Every column that band r's patches at section k take from band r - 2 lies in the cyclic run of 8 columns from far_start[k, r - 2, 0], and every column taken from band r + 2 in the run from far_start[k, r + 2, 1]. stencil_base[k, 0] is at most 28 and stencil_base[k, 1] at most 12.
All inputs are finite; a program needn't handle non-finite values.
Results may differ from the reference program's by a relative error of at most 0.001.
Values may be sent and summed in bfloat16 or wider, within the bound.
No kernel may reach another device: no remote copies, remote signals or barrier semaphores. Data moves between devices by JAX's collectives and lax.ppermute only.
A program may use at most 64 MiB of HBM per device.

```python
import jax
import jax.numpy as jnp
from jax import lax

TRACERS = 8
ITERS = 3
BW = 16
BH = 8
BLOCKS_DEV = 16
BLK = 128
SECTIONS = 4
LEVELS = 32
NBLK = 1024
N_TILE = 64


def band_plan(key):
    nblocks = BLOCKS_DEV
    half_run = nblocks // 2
    subkeys = jax.random.split(key, 4)
    shifts = jax.random.randint(subkeys[0], (SECTIONS, N_TILE, 1), 0, nblocks)
    anchor = jax.random.randint(subkeys[1], (SECTIONS, N_TILE, 1), 0, nblocks)
    anchor = anchor.at[0, 0, 0].set((nblocks - 1 - shifts[0, 0, 0]) % nblocks)
    anchor = anchor.at[0, 1, 0].set((nblocks - shifts[0, 1, 0]) % nblocks)
    jet_side = jax.random.randint(subkeys[2], (SECTIONS, N_TILE, 1), 0, 2)
    near_offset = jax.random.randint(subkeys[3], (SECTIONS, N_TILE, nblocks), -1, 1)
    column = jnp.arange(nblocks, dtype=jnp.int32)[None, None, :]
    far_block = (column - anchor) % nblocks < half_run - 1
    offset = jnp.where(far_block, jnp.where(jet_side == 0, -2, 1), near_offset)
    band_ids = jnp.arange(N_TILE, dtype=jnp.int32)[None, :, None]
    upper_band = jnp.clip(band_ids + offset, 0, N_TILE - 2)
    left_col = (column + shifts) % nblocks
    region_table = jnp.stack([upper_band, left_col], axis=-1).reshape(SECTIONS, N_TILE * nblocks, 2)
    run_start = ((anchor + shifts) % nblocks)[:, :, 0]
    toward_high = jnp.roll(run_start, -2, axis=1)
    toward_low = jnp.roll(run_start, 2, axis=1)
    far_table = jnp.stack([toward_high, toward_low], axis=-1)
    return (region_table.astype(jnp.int32), far_table.astype(jnp.int32))


def draw_regions(key, part):
    region_table, far_table = band_plan(jax.random.fold_in(key, 11))
    return region_table


def draw_far_start(key, part):
    region_table, far_table = band_plan(jax.random.fold_in(key, 11))
    return far_table


def draw_stencil_base(key, part):
    subkeys = jax.random.split(jax.random.fold_in(key, 23), 2)
    column_base = jax.random.randint(subkeys[0], (SECTIONS, 1, N_TILE * BLOCKS_DEV, BW * BH), 0, 2 * BW - 3)
    row_base = jax.random.randint(subkeys[1], (SECTIONS, 1, N_TILE * BLOCKS_DEV, BW * BH), 0, 2 * BH - 3)
    return jnp.concatenate([column_base, row_base], axis=1).astype(jnp.int32)


def block_scale(key, extent, pieces, smallest, high):
    def one(axis_at, blocks):
        draws = jax.random.uniform(jax.random.fold_in(jax.random.fold_in(key, 6), axis_at), (blocks,), jnp.float32, smallest / len(pieces), high / len(pieces))
        return jnp.repeat(jnp.exp(draws), extent[axis_at] // blocks).reshape((-1,) + (1,) * (len(extent) - axis_at - 1))

    level = one(*pieces[0])
    for cut in pieces[1:]:
        level = level * one(*cut)
    return level


def centred(own_key, shape, spread, limit, shards=(), held_as=jnp.bfloat16):
    values = spread * jax.random.normal(own_key, shape, jnp.float32)
    if shards:
        values = values * block_scale(own_key, shape, shards, -0.22, 0.18)
    return jnp.clip(values, -limit, limit).astype(held_as)


def setup_inputs(seed: int = 0) -> dict:
    splits = jax.random.split(jax.random.key(seed), 6)
    return {
        "tracers": centred(splits[0], (TRACERS, LEVELS, NBLK, BLK), 1.0, 6.0, ((1, 8), (2, 64))),
        "wind_field": centred(splits[1], (3, LEVELS, NBLK, BLK), 1.0, 5.0, ((1, 8), (2, 64))),
        "regions": draw_regions(jax.random.fold_in(splits[5], 71), 0),
        "stencil_base": draw_stencil_base(jax.random.fold_in(splits[5], 71), 0),
        "far_start": draw_far_start(jax.random.fold_in(splits[5], 71), 0),
    }


def lagrange_cubic(position):
    return [
        -(position - 1.0) * (position - 2.0) * (position - 3.0) / 6.0,
        position * (position - 2.0) * (position - 3.0) / 2.0,
        -position * (position - 1.0) * (position - 3.0) / 2.0,
        position * (position - 1.0) * (position - 2.0) / 6.0,
    ]


def wind_points():
    return [(1, 1), (2, 1), (1, 2), (2, 2)]


def cubic_points():
    listed = []
    for row_step in range(4):
        for column_step in range(4):
            listed.append((column_step, row_step))
    return listed


def patch_index(region_rows, base_rows, own_band, starts, nblocks, points):
    half_run = nblocks // 2
    upper_band = region_rows[:, 0][:, None]
    left_col = region_rows[:, 1][:, None]
    indexes = []
    insides = []
    for column_step, row_step in points:
        column_x = base_rows[0] + column_step
        row_y = base_rows[1] + row_step
        point_band = upper_band + row_y // BH
        point_col = (left_col + column_x // BW) % nblocks
        cell_in = (row_y % BH) * BW + column_x % BW
        offset_band = point_band - own_band
        run_low = (point_col - starts[0]) % nblocks
        run_high = (point_col - starts[1]) % nblocks
        inside = jnp.where(offset_band == -2, run_low < half_run, jnp.where(offset_band == 2, run_high < half_run, True))
        indexes.append(((point_band * nblocks + point_col) * (BW * BH) + cell_in).reshape(-1).astype(jnp.int32))
        insides.append(inside.astype(jnp.float32).reshape(-1))
    return jnp.stack(indexes), jnp.stack(insides)


def reference(tracers, wind_field, regions, stencil_base, far_start):
    n_tracer = tracers.shape[0]
    n_level = tracers.shape[1]
    nblocks = BLOCKS_DEV
    cells_blk = BW * BH
    band_cells = nblocks * cells_blk
    tracer_flat = tracers.reshape(n_tracer, n_level, N_TILE * band_cells)
    wind_flat = wind_field.reshape(3, n_level, N_TILE * band_cells)

    def one_band(own_band):
        first_block = own_band * nblocks
        arrive = lax.dynamic_slice_in_dim(wind_flat, own_band * band_cells, band_cells, 2).astype(jnp.float32)
        displace = jnp.zeros((3, n_level, band_cells), jnp.float32)
        renewed = None
        for section_idx in range(ITERS + 1):
            region_rows = lax.dynamic_slice_in_dim(regions[section_idx], first_block, nblocks, 0)
            base_rows = lax.dynamic_slice_in_dim(stencil_base[section_idx], first_block, nblocks, 1)
            starts = (far_start[section_idx, jnp.maximum(own_band - 2, 0), 0],
                      far_start[section_idx, jnp.minimum(own_band + 2, N_TILE - 1), 1])
            if section_idx < ITERS:
                index_all, inside_all = patch_index(region_rows, base_rows, own_band, starts, nblocks, wind_points())
                gathered = jnp.take(wind_flat, index_all, axis=2, mode="clip")
                frac_x = 0.5 + 0.5 * jnp.tanh(displace[0])
                frac_y = 0.5 + 0.5 * jnp.tanh(displace[1])
                midwind = jnp.zeros((3, n_level, band_cells), jnp.float32)
                for point_idx, (column_step, row_step) in enumerate(wind_points()):
                    weight_x = frac_x if column_step == 2 else 1.0 - frac_x
                    weight_y = frac_y if row_step == 2 else 1.0 - frac_y
                    factor = weight_x * weight_y * inside_all[point_idx]
                    midwind = midwind + factor[None] * gathered[:, :, point_idx].astype(jnp.float32)
                displace = 0.5 * (arrive + midwind)
            else:
                index_all, inside_all = patch_index(region_rows, base_rows, own_band, starts, nblocks, cubic_points())
                gathered = jnp.take(tracer_flat, index_all, axis=2, mode="clip")
                extended = jnp.concatenate([gathered[:, :1], gathered, gathered[:, -1:]], axis=1)
                weight_x = lagrange_cubic(1.5 + 0.5 * jnp.tanh(displace[0]))
                weight_y = lagrange_cubic(1.5 + 0.5 * jnp.tanh(displace[1]))
                factors = []
                for point_idx, (column_step, row_step) in enumerate(cubic_points()):
                    factors.append(weight_x[column_step] * weight_y[row_step] * inside_all[point_idx])
                horizontal = jnp.stack(factors, axis=1)
                vertical = jnp.tanh(displace[2])
                level_weights = [0.5 * vertical * (vertical - 1.0), 1.0 - vertical * vertical, 0.5 * vertical * (vertical + 1.0)]
                summed = jnp.zeros((n_tracer, n_level, band_cells), jnp.float32)
                for level_step in range(3):
                    window = extended[:, level_step:level_step + n_level].astype(jnp.float32)
                    summed = summed + level_weights[level_step][None] * jnp.sum(horizontal[None] * window, axis=2)
                renewed = summed.astype(jnp.bfloat16)
        return renewed, displace

    band_ids = jnp.arange(N_TILE, dtype=jnp.int32)
    renewed, displace = lax.map(one_band, band_ids)
    tracers_new = jnp.transpose(renewed, (1, 2, 0, 3)).reshape(n_tracer, n_level, N_TILE * nblocks, cells_blk)
    displacement = jnp.transpose(displace, (1, 2, 0, 3)).reshape(3, n_level, N_TILE * nblocks, cells_blk)
    return tracers_new, displacement
```

```python
import jax
import jax.numpy as jnp
from jax import lax
from jax.experimental import pallas as pl
from jax.experimental.pallas import tpu as pltpu
from jax.sharding import PartitionSpec as P

ITERS = 3
BW = 16
BH = 8
CELLS = BW * BH
QUADS = 4
POINTS = QUADS * CELLS
N_OFF = 5


def shifted(shard, axis, by):
    devices = lax.axis_size(axis)
    pairs = [(i, i + by) for i in range(devices) if 0 <= i + by < devices]
    return lax.ppermute(shard, axis, pairs)


def lagrange_cubic(position):
    return [
        -(position - 1.0) * (position - 2.0) * (position - 3.0) / 6.0,
        position * (position - 2.0) * (position - 3.0) / 2.0,
        -position * (position - 1.0) * (position - 3.0) / 2.0,
        position * (position - 1.0) * (position - 2.0) / 6.0,
    ]


def selectors(regions, own_band, start_low, start_high, nblocks):
    upper = regions[:, 0:1]
    left = regions[:, 1:2]
    lane = lax.broadcasted_iota(jnp.int32, (nblocks, N_OFF * nblocks), 1)
    rows = []
    for quad_y in (0, 1):
        for quad_x in (0, 1):
            offset = upper + (quad_y - own_band)
            col = (left + quad_x) & (nblocks - 1)
            run_low = (col - start_low) & (nblocks - 1)
            run_high = (col - start_high) & (nblocks - 1)
            run = jnp.where(offset == -2, run_low, jnp.where(offset == 2, run_high, 0))
            slot = jnp.where(run < nblocks // 2, (offset + 2) * nblocks + col, -1)
            rows.append(jnp.where(lane == slot, 1.0, 0.0).astype(jnp.bfloat16))
    return jnp.concatenate(rows, axis=0)


def class_order(log_step):
    step = 1 << log_step
    mask = step - 1
    source = lax.broadcasted_iota(jnp.int32, (POINTS, 128), 0)
    lane = lax.broadcasted_iota(jnp.int32, (POINTS, 128), 1)
    x = (source & (BW - 1)) + ((source >> 7) & 1) * BW
    y = ((source >> 4) & (BH - 1)) + (source >> 8) * BH
    kind = (y & mask) * step + (x & mask)
    place = (y >> log_step) * (2 * BW // step) + (x >> log_step)
    dest = kind * (POINTS // (step * step)) + place
    cols = [
        jnp.where(dest == lane + v * 128, 1.0, 0.0).astype(jnp.bfloat16) for v in range(QUADS)
    ]
    return jnp.concatenate(cols, axis=1)


def sort_rows(picked, nblocks, lanes_at):
    return jnp.concatenate(
        [
            picked[q * nblocks : (q + 1) * nblocks, lanes_at : lanes_at + CELLS]
            for q in range(QUADS)
        ],
        axis=1,
    )


def take_lanes(values, index):
    return jnp.take_along_axis(values, index, axis=1, mode="promise_in_bounds")


def wind_kernel(
    own_ref, far_ref, regions_ref, base_ref, lo2, lo1, mid, hi1, hi2, out_ref, rows_ref, patch_ref
):
    n_comp, n_level, nblocks, _ = out_ref.shape
    n_bands = far_ref.shape[1]
    own = own_ref[0]
    low_at = jnp.maximum(own - 2, 0)
    high_at = jnp.minimum(own + 2, n_bands - 1)
    pick = jnp.concatenate(
        [
            selectors(regions_ref[k], own, far_ref[k, low_at, 0], far_ref[k, high_at, 1], nblocks)
            for k in range(ITERS)
        ],
        axis=0,
    )
    bands = (lo2, lo1, mid, hi1, hi2)
    fields = [(c, l) for c in range(n_comp) for l in range(n_level)]
    for i in range(0, len(fields), 2):
        pair = [
            jnp.concatenate([b[c, l] for b in bands], axis=0) for c, l in fields[i : i + 2]
        ]
        picked = jnp.dot(
            pick, jnp.concatenate(pair, axis=1), preferred_element_type=jnp.float32
        ).astype(jnp.bfloat16)
        for k in range(ITERS):
            part = picked[k * QUADS * nblocks : (k + 1) * QUADS * nblocks]
            for half in range(2):
                at = (k * len(fields) + i + half) * nblocks
                rows_ref[at : at + nblocks, :] = sort_rows(part, nblocks, half * CELLS)
    patch_ref[...] = jnp.dot(rows_ref[...], class_order(1), preferred_element_type=jnp.float32)
    for h in range(0, nblocks, 8):
        displace = None
        for k in range(ITERS):
            x0 = base_ref[k, 0, h : h + 8, :] + 1
            y0 = base_ref[k, 1, h : h + 8, :] + 1
            xs = [(x0 + 1) >> 1, x0 >> 1]
            ys = [((y0 + 1) >> 1) * BW, (y0 >> 1) * BW]
            index = [[ys[ry] + xs[rx] for rx in range(2)] for ry in range(2)]
            odd_x = (x0 & 1) == 1
            odd_y = (y0 & 1) == 1
            after = []
            for l in range(n_level):
                if displace is None:
                    frac_x = jnp.full(x0.shape, 0.5, jnp.float32)
                    frac_y = frac_x
                else:
                    frac_x = 0.5 + 0.5 * jnp.tanh(displace[l][0])
                    frac_y = 0.5 + 0.5 * jnp.tanh(displace[l][1])
                weight_x = [
                    jnp.where(odd_x, frac_x, 1.0 - frac_x),
                    jnp.where(odd_x, 1.0 - frac_x, frac_x),
                ]
                weight_y = [
                    jnp.where(odd_y, frac_y, 1.0 - frac_y),
                    jnp.where(odd_y, 1.0 - frac_y, frac_y),
                ]
                weight = [[weight_x[rx] * weight_y[ry] for rx in range(2)] for ry in range(2)]
                comps = []
                for c in range(n_comp):
                    at = (k * len(fields) + c * n_level + l) * nblocks + h
                    total = None
                    for ry in range(2):
                        for rx in range(2):
                            kind = ry * 2 + rx
                            values = patch_ref[at : at + 8, kind * 128 : (kind + 1) * 128]
                            term = weight[ry][rx] * take_lanes(values, index[ry][rx])
                            total = term if total is None else total + term
                    arrive = mid[c, l, h : h + 8, :].astype(jnp.float32)
                    comps.append(0.5 * (arrive + total))
                after.append(comps)
            displace = after
        for l in range(n_level):
            for c in range(n_comp):
                out_ref[c, l, h : h + 8, :] = displace[l][c]


def tracer_kernel(
    own_ref,
    far_ref,
    regions_ref,
    base_ref,
    displace_ref,
    below_ref,
    above_ref,
    lo2,
    lo1,
    mid,
    hi1,
    hi2,
    out_ref,
    rows_ref,
    patch_ref,
    weight_ref,
):
    n_tracer, n_level, nblocks, _ = out_ref.shape
    n_ext = n_level + 2
    n_bands = far_ref.shape[1]
    first = lo2.shape[0] - n_tracer
    own = own_ref[0]
    at_bottom = own_ref[1] == 0
    at_top = own_ref[1] == own_ref[2] - 1
    low_at = jnp.maximum(own - 2, 0)
    high_at = jnp.minimum(own + 2, n_bands - 1)
    k = ITERS
    pick = selectors(regions_ref[k], own, far_ref[k, low_at, 0], far_ref[k, high_at, 1], nblocks)
    bands = (lo2, lo1, mid, hi1, hi2)
    for t in range(n_tracer):
        levels = [
            jnp.concatenate([b[first + t, l] for b in bands], axis=0) for l in range(n_level)
        ]
        bottom = jnp.where(at_bottom, levels[0], below_ref[t])
        top = jnp.where(at_top, levels[-1], above_ref[t])
        levels = [bottom] + levels + [top]
        for e in range(0, n_ext, 2):
            picked = jnp.dot(
                pick,
                jnp.concatenate(levels[e : e + 2], axis=1),
                preferred_element_type=jnp.float32,
            ).astype(jnp.bfloat16)
            for half in range(2):
                at = (t * n_ext + e + half) * nblocks
                rows_ref[at : at + nblocks, :] = sort_rows(picked, nblocks, half * CELLS)
    patch_ref[...] = jnp.dot(rows_ref[...], class_order(2), preferred_element_type=jnp.float32)
    for h in range(0, nblocks, 8):
        x0 = base_ref[k, 0, h : h + 8, :]
        y0 = base_ref[k, 1, h : h + 8, :]
        xs = [((x0 + ((r - x0) & 3)) >> 2) + r * 32 for r in range(4)]
        ys = [((y0 + ((r - y0) & 3)) >> 2) * 8 for r in range(4)]
        index = [[ys[ry] + xs[rx] for rx in range(4)] for ry in range(4)]
        layers = []
        for l in range(n_level):
            split = []
            for axis, start in ((0, x0), (1, y0)):
                w = lagrange_cubic(1.5 + 0.5 * jnp.tanh(displace_ref[axis, l, h : h + 8, :]))
                bit0 = (start & 1) == 1
                bit1 = (start & 2) == 2
                w = [jnp.where(bit0, w[(r - 1) & 3], w[r]) for r in range(4)]
                w = [jnp.where(bit1, w[(r - 2) & 3], w[r]) for r in range(4)]
                split.append(w)
            for ry in range(4):
                for rx in range(4):
                    weight_ref[l, ry * 4 + rx] = split[0][rx] * split[1][ry]
            s = jnp.tanh(displace_ref[2, l, h : h + 8, :])
            layers.append([0.5 * s * (s - 1.0), 1.0 - s * s, 0.5 * s * (s + 1.0)])

        def one_tracer(t, carry):
            totals = [None] * n_level
            for e in range(n_ext):
                at = pl.multiple_of((t * n_ext + e) * nblocks + h, 8)
                taken = []
                for ry in range(4):
                    values = patch_ref[pl.ds(at, 8), ry * 128 : (ry + 1) * 128]
                    for rx in range(4):
                        taken.append(take_lanes(values, index[ry][rx]))
                for l in range(n_level):
                    d = e - l
                    if 0 <= d <= 2:
                        acc = weight_ref[l, 0] * taken[0]
                        for kind in range(1, 16):
                            acc = acc + weight_ref[l, kind] * taken[kind]
                        acc = layers[l][d] * acc
                        totals[l] = acc if totals[l] is None else totals[l] + acc
            for l in range(n_level):
                out_ref[t, l, h : h + 8, :] = totals[l].astype(jnp.bfloat16)
            return carry

        lax.fori_loop(0, n_tracer, one_tracer, 0)


def body(tracers, wind_field, regions, stencil_base, far_start):
    n_tracer, n_level, nblocks, cells = tracers.shape
    own_band = lax.axis_index("tile")
    level_pos = lax.axis_index("lev")
    place = jnp.stack([own_band, level_pos, jnp.int32(lax.axis_size("lev"))]).astype(jnp.int32)
    packet = jnp.concatenate([wind_field, tracers], axis=0)
    lo1 = shifted(packet, "tile", 1)
    hi1 = shifted(packet, "tile", -1)
    lo2 = shifted(packet, "tile", 2)
    hi2 = shifted(packet, "tile", -2)
    bands = (lo2, lo1, packet, hi1, hi2)
    smem = pl.BlockSpec(memory_space=pltpu.SMEM)
    vmem = pl.BlockSpec(memory_space=pltpu.VMEM)
    params = pltpu.CompilerParams(vmem_limit_bytes=40 * 1024 * 1024)
    tops = jnp.concatenate([b[3:, n_level - 1] for b in bands], axis=1)
    bottoms = jnp.concatenate([b[3:, 0] for b in bands], axis=1)
    below = shifted(tops, "lev", 1)
    above = shifted(bottoms, "lev", -1)
    displacement = pl.pallas_call(
        wind_kernel,
        name="wind",
        out_shape=jax.ShapeDtypeStruct((3, n_level, nblocks, cells), jnp.float32),
        in_specs=[smem, smem] + [vmem] * 7,
        out_specs=vmem,
        scratch_shapes=[
            pltpu.VMEM((ITERS * 3 * n_level * nblocks, POINTS), jnp.bfloat16),
            pltpu.VMEM((ITERS * 3 * n_level * nblocks, POINTS), jnp.float32),
        ],
        compiler_params=params,
    )(place, far_start, regions, stencil_base, *bands)
    rows = n_tracer * (n_level + 2) * nblocks
    tracers_new = pl.pallas_call(
        tracer_kernel,
        name="tracer",
        out_shape=jax.ShapeDtypeStruct(tracers.shape, jnp.bfloat16),
        in_specs=[smem, smem] + [vmem] * 10,
        out_specs=vmem,
        scratch_shapes=[
            pltpu.VMEM((rows, POINTS), jnp.bfloat16),
            pltpu.VMEM((rows, POINTS), jnp.float32),
            pltpu.VMEM((n_level, 16, 8, 128), jnp.float32),
        ],
        compiler_params=params,
    )(place, far_start, regions, stencil_base, displacement, below, above, *bands)
    return (tracers_new, displacement)


def solution(mesh):
    return jax.shard_map(
        body,
        mesh=mesh,
        in_specs=(
            P(None, "lev", "tile", None),
            P(None, "lev", "tile", None),
            P(None, "tile", None),
            P(None, None, "tile", None),
            P(),
        ),
        out_specs=(P(None, "lev", "tile", None), P(None, "lev", "tile", None)),
        check_vma=False,
    )
```

```python
import jax
import jax.numpy as jnp
from jax import lax
from jax.experimental import pallas as pl
from jax.experimental.pallas import tpu as pltpu
from jax.sharding import PartitionSpec as P

ITERS = 3
BW = 16
BH = 8
CELLS = BW * BH
QUADS = 4
POINTS = QUADS * CELLS
N_OFF = 5


def shifted(shard, axis, by):
    devices = lax.axis_size(axis)
    pairs = [(i, i + by) for i in range(devices) if 0 <= i + by < devices]
    return lax.ppermute(shard, axis, pairs)


def lagrange_cubic(position):
    return [
        -(position - 1.0) * (position - 2.0) * (position - 3.0) / 6.0,
        position * (position - 2.0) * (position - 3.0) / 2.0,
        -position * (position - 1.0) * (position - 3.0) / 2.0,
        position * (position - 1.0) * (position - 2.0) / 6.0,
    ]


def selectors(regions, own_band, start_low, start_high, nblocks):
    upper = regions[:, 0:1]
    left = regions[:, 1:2]
    lane = lax.broadcasted_iota(jnp.int32, (nblocks, N_OFF * nblocks), 1)
    rows = []
    for quad_y in (0, 1):
        for quad_x in (0, 1):
            offset = upper + (quad_y - own_band)
            col = (left + quad_x) & (nblocks - 1)
            run_low = (col - start_low) & (nblocks - 1)
            run_high = (col - start_high) & (nblocks - 1)
            run = jnp.where(offset == -2, run_low, jnp.where(offset == 2, run_high, 0))
            slot = jnp.where(run < nblocks // 2, (offset + 2) * nblocks + col, -1)
            rows.append(jnp.where(lane == slot, 1.0, 0.0).astype(jnp.bfloat16))
    return jnp.concatenate(rows, axis=0)


def class_order(log_step):
    step = 1 << log_step
    mask = step - 1
    source = lax.broadcasted_iota(jnp.int32, (POINTS, 128), 0)
    lane = lax.broadcasted_iota(jnp.int32, (POINTS, 128), 1)
    x = (source & (BW - 1)) + ((source >> 7) & 1) * BW
    y = ((source >> 4) & (BH - 1)) + (source >> 8) * BH
    kind = (y & mask) * step + (x & mask)
    place = (y >> log_step) * (2 * BW // step) + (x >> log_step)
    dest = kind * (POINTS // (step * step)) + place
    cols = [
        jnp.where(dest == lane + v * 128, 1.0, 0.0).astype(jnp.bfloat16) for v in range(QUADS)
    ]
    return jnp.concatenate(cols, axis=1)


def sort_rows(picked, nblocks, lanes_at):
    return jnp.concatenate(
        [
            picked[q * nblocks : (q + 1) * nblocks, lanes_at : lanes_at + CELLS]
            for q in range(QUADS)
        ],
        axis=1,
    )


LANES = lax.GatherDimensionNumbers(
    offset_dims=(),
    collapsed_slice_dims=(1,),
    start_index_map=(1,),
    operand_batching_dims=(0,),
    start_indices_batching_dims=(0,),
)


def take_lanes(values, index):
    picked = lax.gather(
        values,
        index[..., None],
        LANES,
        slice_sizes=(1, 1),
        mode=lax.GatherScatterMode.PROMISE_IN_BOUNDS,
    )
    return picked.astype(jnp.float32)


def wind_kernel(
    own_ref, regions_ref, base_ref, lo2, lo1, mid, hi1, hi2, out_ref, rows_ref, patch_ref
):
    n_comp, n_level, nblocks, _ = out_ref.shape
    own = own_ref[0]
    pick = jnp.concatenate(
        [
            selectors(regions_ref[k], own, own_ref[3 + 2 * k], own_ref[4 + 2 * k], nblocks)
            for k in range(ITERS)
        ],
        axis=0,
    )
    bands = (lo2, lo1, mid, hi1, hi2)
    fields = [(c, l) for c in range(n_comp) for l in range(n_level)]
    for i in range(0, len(fields), 2):
        pair = [
            jnp.concatenate([b[c, l] for b in bands], axis=0) for c, l in fields[i : i + 2]
        ]
        picked = jnp.dot(
            pick, jnp.concatenate(pair, axis=1), preferred_element_type=jnp.float32
        ).astype(jnp.bfloat16)
        for k in range(ITERS):
            part = picked[k * QUADS * nblocks : (k + 1) * QUADS * nblocks]
            for half in range(2):
                at = (k * len(fields) + i + half) * nblocks
                rows_ref[at : at + nblocks, :] = sort_rows(part, nblocks, half * CELLS)
    patch_ref[...] = jnp.dot(
        rows_ref[...], class_order(1), preferred_element_type=jnp.float32
    ).astype(jnp.bfloat16)
    displace = [[None] * n_comp for _ in range(n_level)]
    for k in range(ITERS):
        x0 = base_ref[k, 0] + 1
        y0 = base_ref[k, 1] + 1
        xs = [(x0 + 1) >> 1, x0 >> 1]
        ys = [((y0 + 1) >> 1) * BW, (y0 >> 1) * BW]
        index = [[(ys[ry] + xs[rx]).astype(jnp.int16) for rx in range(2)] for ry in range(2)]
        odd_x = (x0 & 1) == 1
        odd_y = (y0 & 1) == 1
        taken = {}
        for ry in range(2):
            for rx in range(2):
                kind = ry * 2 + rx
                for i in range(len(fields)):
                    at = (k * len(fields) + i) * nblocks
                    values = patch_ref[at : at + nblocks, kind * 128 : (kind + 1) * 128]
                    taken[i, kind] = take_lanes(values, index[ry][rx])
        for l in range(n_level):
            if k == 0:
                frac_x = jnp.full(x0.shape, 0.5, jnp.float32)
                frac_y = frac_x
            else:
                frac_x = 0.5 + 0.5 * jnp.tanh(displace[l][0])
                frac_y = 0.5 + 0.5 * jnp.tanh(displace[l][1])
            weight_x = [
                jnp.where(odd_x, frac_x, 1.0 - frac_x),
                jnp.where(odd_x, 1.0 - frac_x, frac_x),
            ]
            weight_y = [
                jnp.where(odd_y, frac_y, 1.0 - frac_y),
                jnp.where(odd_y, 1.0 - frac_y, frac_y),
            ]
            for c in range(n_comp):
                total = None
                for ry in range(2):
                    for rx in range(2):
                        term = weight_x[rx] * weight_y[ry] * taken[c * n_level + l, ry * 2 + rx]
                        total = term if total is None else total + term
                displace[l][c] = 0.5 * (mid[c, l].astype(jnp.float32) + total)
    for l in range(n_level):
        for c in range(n_comp):
            out_ref[c, l] = displace[l][c]


def tracer_kernel(
    own_ref,
    regions_ref,
    base_ref,
    displace_ref,
    below_ref,
    above_ref,
    lo2,
    lo1,
    mid,
    hi1,
    hi2,
    out_ref,
    rows_ref,
    patch_ref,
    weight_ref,
    layer_ref,
):
    n_tracer, n_level, nblocks, _ = out_ref.shape
    n_ext = n_level + 2
    first = lo2.shape[0] - n_tracer
    own = own_ref[0]
    at_bottom = own_ref[1] == 0
    at_top = own_ref[1] == own_ref[2] - 1
    k = ITERS
    pick = selectors(regions_ref[k], own, own_ref[3 + 2 * k], own_ref[4 + 2 * k], nblocks)
    bands = (lo2, lo1, mid, hi1, hi2)
    for t in range(n_tracer):
        levels = [
            jnp.concatenate([b[first + t, l] for b in bands], axis=0) for l in range(n_level)
        ]
        bottom = jnp.where(at_bottom, levels[0], below_ref[t])
        top = jnp.where(at_top, levels[-1], above_ref[t])
        levels = [bottom] + levels + [top]
        for e in range(0, n_ext, 2):
            picked = jnp.dot(
                pick,
                jnp.concatenate(levels[e : e + 2], axis=1),
                preferred_element_type=jnp.float32,
            ).astype(jnp.bfloat16)
            for half in range(2):
                at = (t * n_ext + e + half) * nblocks
                rows_ref[at : at + nblocks, :] = sort_rows(picked, nblocks, half * CELLS)
    patch_ref[...] = jnp.dot(
        rows_ref[...], class_order(2), preferred_element_type=jnp.float32
    ).astype(jnp.bfloat16)
    x0 = base_ref[k, 0]
    y0 = base_ref[k, 1]
    xs = [((x0 + ((r - x0) & 3)) >> 2) + r * 32 for r in range(4)]
    ys = [((y0 + ((r - y0) & 3)) >> 2) * 8 for r in range(4)]
    index = [(ys[ry] + xs[rx]).astype(jnp.int16) for ry in range(4) for rx in range(4)]
    for l in range(n_level):
        split = []
        for axis, start in ((0, x0), (1, y0)):
            w = lagrange_cubic(1.5 + 0.5 * jnp.tanh(displace_ref[axis, l]))
            bit0 = (start & 1) == 1
            bit1 = (start & 2) == 2
            w = [jnp.where(bit0, w[(r - 1) & 3], w[r]) for r in range(4)]
            w = [jnp.where(bit1, w[(r - 2) & 3], w[r]) for r in range(4)]
            split.append(w)
        for ry in range(4):
            for rx in range(4):
                weight_ref[ry * 4 + rx, l] = split[0][rx] * split[1][ry]
        s = jnp.tanh(displace_ref[2, l])
        layer_ref[l, 0] = 0.5 * s * (s - 1.0)
        layer_ref[l, 1] = 1.0 - s * s
        layer_ref[l, 2] = 0.5 * s * (s + 1.0)

    def one_tracer(t, carry):
        sums = {}
        for kind in range(16):
            at_lane = (kind // 4) * 128
            taken = []
            for e in range(n_ext):
                at = pl.multiple_of((t * n_ext + e) * nblocks, nblocks)
                values = patch_ref[pl.ds(at, nblocks), at_lane : at_lane + 128]
                taken.append(take_lanes(values, index[kind]))
            for l in range(n_level):
                weight = weight_ref[kind, l]
                for d in range(3):
                    term = weight * taken[l + d]
                    sums[l, d] = sums[l, d] + term if kind else term
        for l in range(n_level):
            total = layer_ref[l, 0] * sums[l, 0]
            total = total + layer_ref[l, 1] * sums[l, 1] + layer_ref[l, 2] * sums[l, 2]
            out_ref[t, l] = total.astype(jnp.bfloat16)
        return carry

    lax.fori_loop(0, n_tracer, one_tracer, 0)


def body(tracers, wind_field, regions, stencil_base, far_start):
    n_tracer, n_level, nblocks, cells = tracers.shape
    own_band = lax.axis_index("tile")
    level_pos = lax.axis_index("lev")
    n_bands = lax.axis_size("tile")
    starts = jnp.stack(
        [
            far_start[:, jnp.maximum(own_band - 2, 0), 0],
            far_start[:, jnp.minimum(own_band + 2, n_bands - 1), 1],
        ],
        axis=1,
    )
    ranks = jnp.stack([own_band, level_pos, jnp.int32(lax.axis_size("lev"))]).astype(jnp.int32)
    place = jnp.concatenate([ranks, starts.reshape(-1)])
    packet = jnp.concatenate([wind_field, tracers], axis=0)
    lo1 = shifted(packet, "tile", 1)
    hi1 = shifted(packet, "tile", -1)
    lo2 = shifted(packet, "tile", 2)
    hi2 = shifted(packet, "tile", -2)
    bands = (lo2, lo1, packet, hi1, hi2)
    smem = pl.BlockSpec(memory_space=pltpu.SMEM)
    vmem = pl.BlockSpec(memory_space=pltpu.VMEM)
    params = pltpu.CompilerParams(vmem_limit_bytes=40 * 1024 * 1024)
    tops = jnp.concatenate([b[3:, n_level - 1] for b in bands], axis=1)
    bottoms = jnp.concatenate([b[3:, 0] for b in bands], axis=1)
    below = shifted(tops, "lev", 1)
    above = shifted(bottoms, "lev", -1)
    displacement = pl.pallas_call(
        wind_kernel,
        name="wind",
        out_shape=jax.ShapeDtypeStruct((3, n_level, nblocks, cells), jnp.float32),
        in_specs=[smem] + [vmem] * 7,
        out_specs=vmem,
        scratch_shapes=[
            pltpu.VMEM((ITERS * 3 * n_level * nblocks, POINTS), jnp.bfloat16),
            pltpu.VMEM((ITERS * 3 * n_level * nblocks, POINTS), jnp.bfloat16),
        ],
        compiler_params=params,
    )(place, regions, stencil_base, *bands)
    rows = n_tracer * (n_level + 2) * nblocks
    tracers_new = pl.pallas_call(
        tracer_kernel,
        name="tracer",
        out_shape=jax.ShapeDtypeStruct(tracers.shape, jnp.bfloat16),
        in_specs=[smem] + [vmem] * 10,
        out_specs=vmem,
        scratch_shapes=[
            pltpu.VMEM((rows, POINTS), jnp.bfloat16),
            pltpu.VMEM((rows, POINTS), jnp.bfloat16),
            pltpu.VMEM((16, n_level, nblocks, cells), jnp.float32),
            pltpu.VMEM((n_level, 3, nblocks, cells), jnp.float32),
        ],
        compiler_params=params,
    )(place, regions, stencil_base, displacement, below, above, *bands)
    return (tracers_new, displacement)


def solution(mesh):
    return jax.shard_map(
        body,
        mesh=mesh,
        in_specs=(
            P(None, "lev", "tile", None),
            P(None, "lev", "tile", None),
            P(None, "tile", None),
            P(None, None, "tile", None),
            P(),
        ),
        out_specs=(P(None, "lev", "tile", None), P(None, "lev", "tile", None)),
        check_vma=False,
    )
```

```python
import jax
import jax.numpy as jnp
from jax import lax
from jax.experimental import pallas as pl
from jax.experimental.pallas import tpu as pltpu
from jax.sharding import PartitionSpec as P

ITERS = 3
BW = 16
BH = 8
CELLS = BW * BH
QUADS = 4
POINTS = QUADS * CELLS
N_OFF = 5


def shifted(shard, axis, by):
    devices = lax.axis_size(axis)
    pairs = [(i, i + by) for i in range(devices) if 0 <= i + by < devices]
    return lax.ppermute(shard, axis, pairs)


def lagrange_cubic(position):
    return [
        -(position - 1.0) * (position - 2.0) * (position - 3.0) / 6.0,
        position * (position - 2.0) * (position - 3.0) / 2.0,
        -position * (position - 1.0) * (position - 3.0) / 2.0,
        position * (position - 1.0) * (position - 2.0) / 6.0,
    ]


def column(row, count):
    at = lax.broadcasted_iota(jnp.int32, (count, count), 0)
    lane = lax.broadcasted_iota(jnp.int32, (count, count), 1)
    return jnp.sum(jnp.where(at == lane, row, 0), axis=1, keepdims=True)


def selectors(regions, starts, own_band, nblocks):
    upper = column(regions[0:1], nblocks)
    left = column(regions[1:2], nblocks)
    mate = jnp.where((own_band & 1) == 0, 1, -1)
    lane = lax.broadcasted_iota(jnp.int32, (nblocks, N_OFF * nblocks), 1)
    rows = []
    for quad_y in (0, 1):
        for quad_x in (0, 1):
            offset = upper + (quad_y - own_band)
            col = (left + quad_x) & (nblocks - 1)
            run_low = (col - starts[0]) & (nblocks - 1)
            run_high = (col - starts[1]) & (nblocks - 1)
            run = jnp.where(offset == -2, run_low, jnp.where(offset == 2, run_high, 0))
            place = jnp.where(offset == mate, 1, jnp.where(offset == -mate, 3, offset + 2))
            slot = jnp.where(run < nblocks // 2, place * nblocks + col, -1)
            rows.append(jnp.where(lane == slot, 1.0, 0.0).astype(jnp.bfloat16))
    return jnp.concatenate(rows, axis=0)


def run_starts(far, own_band):
    n_bands = far.shape[1]
    lane = lax.broadcasted_iota(jnp.int32, (1, n_bands), 1)
    picked = []
    for side, band in ((0, own_band - 2), (1, own_band + 2)):
        band = jnp.clip(band, 0, n_bands - 1)
        picked.append(
            jnp.sum(jnp.where(lane == band, far[side : side + 1], 0), axis=1, keepdims=True)
        )
    return picked


def class_order(log_step):
    step = 1 << log_step
    mask = step - 1
    source = lax.broadcasted_iota(jnp.int32, (POINTS, 128), 0)
    lane = lax.broadcasted_iota(jnp.int32, (POINTS, 128), 1)
    x = (source & (BW - 1)) + ((source >> 7) & 1) * BW
    y = ((source >> 4) & (BH - 1)) + (source >> 8) * BH
    kind = (y & mask) * step + (x & mask)
    place = (y >> log_step) * (2 * BW // step) + (x >> log_step)
    dest = kind * (POINTS // (step * step)) + place
    cols = [
        jnp.where(dest == lane + v * 128, 1.0, 0.0).astype(jnp.bfloat16) for v in range(QUADS)
    ]
    return jnp.concatenate(cols, axis=1)


def sort_rows(picked, nblocks, lanes_at):
    return jnp.concatenate(
        [
            picked[q * nblocks : (q + 1) * nblocks, lanes_at : lanes_at + CELLS]
            for q in range(QUADS)
        ],
        axis=1,
    )


LANES = lax.GatherDimensionNumbers(
    offset_dims=(),
    collapsed_slice_dims=(1,),
    start_index_map=(1,),
    operand_batching_dims=(0,),
    start_indices_batching_dims=(0,),
)


def take_lanes(values, index):
    picked = lax.gather(
        values,
        index[..., None],
        LANES,
        slice_sizes=(1, 1),
        mode=lax.GatherScatterMode.PROMISE_IN_BOUNDS,
    )
    return picked.astype(jnp.float32)


def transport_kernel(
    far_ref,
    regions_ref,
    base_ref,
    mate,
    cross,
    hi2,
    lo2,
    mid,
    new_ref,
    displace_ref,
    wind_rows,
    wind_patch,
    rows_ref,
    patch_ref,
    weight_ref,
    layer_ref,
):
    n_tracer, n_level, nblocks, _ = new_ref.shape
    n_comp = displace_ref.shape[0]
    n_ext = n_level + 2
    own = lax.axis_index("tile")
    level_pos = lax.axis_index("lev")
    at_bottom = level_pos == 0
    at_top = level_pos == lax.axis_size("lev") - 1
    picks = [
        selectors(regions_ref[k], run_starts(far_ref[k], own), own, nblocks)
        for k in range(ITERS + 1)
    ]
    bands = (lo2, mate, mid, cross, hi2)

    def stacked(row):
        return jnp.concatenate([b[row] for b in bands], axis=0)

    n_field = n_comp * n_level
    pick = jnp.concatenate(picks[:ITERS], axis=0)
    for i in range(0, n_field, 2):
        picked = jnp.dot(
            pick,
            jnp.concatenate([stacked(i), stacked(i + 1)], axis=1),
            preferred_element_type=jnp.float32,
        ).astype(jnp.bfloat16)
        for k in range(ITERS):
            part = picked[k * QUADS * nblocks : (k + 1) * QUADS * nblocks]
            for half in range(2):
                at = (k * n_field + i + half) * nblocks
                wind_rows[at : at + nblocks, :] = sort_rows(part, nblocks, half * CELLS)
    wind_patch[...] = jnp.dot(
        wind_rows[...], class_order(1), preferred_element_type=jnp.float32
    ).astype(jnp.bfloat16)
    for t in range(n_tracer):
        levels = [stacked(n_field + t * n_level + l) for l in range(n_level)]
        below = stacked(n_field + n_tracer * n_level + t)
        above = stacked(n_field + n_tracer * (n_level + 1) + t)
        bottom = jnp.where(at_bottom, levels[0], below)
        top = jnp.where(at_top, levels[-1], above)
        levels = [bottom] + levels + [top]
        for e in range(0, n_ext, 2):
            picked = jnp.dot(
                picks[ITERS],
                jnp.concatenate(levels[e : e + 2], axis=1),
                preferred_element_type=jnp.float32,
            ).astype(jnp.bfloat16)
            for half in range(2):
                at = (t * n_ext + e + half) * nblocks
                rows_ref[at : at + nblocks, :] = sort_rows(picked, nblocks, half * CELLS)
    patch_ref[...] = jnp.dot(
        rows_ref[...], class_order(2), preferred_element_type=jnp.float32
    ).astype(jnp.bfloat16)
    displace = [[None] * n_comp for _ in range(n_level)]
    for k in range(ITERS):
        x0 = base_ref[k, 0] + 1
        y0 = base_ref[k, 1] + 1
        xs = [(x0 + 1) >> 1, x0 >> 1]
        ys = [((y0 + 1) >> 1) * BW, (y0 >> 1) * BW]
        index = [[(ys[ry] + xs[rx]).astype(jnp.int16) for rx in range(2)] for ry in range(2)]
        odd_x = (x0 & 1) == 1
        odd_y = (y0 & 1) == 1
        taken = {}
        for ry in range(2):
            for rx in range(2):
                kind = ry * 2 + rx
                for i in range(n_field):
                    at = (k * n_field + i) * nblocks
                    values = wind_patch[at : at + nblocks, kind * 128 : (kind + 1) * 128]
                    taken[i, kind] = take_lanes(values, index[ry][rx])
        for l in range(n_level):
            if k == 0:
                frac_x = jnp.full(x0.shape, 0.5, jnp.float32)
                frac_y = frac_x
            else:
                frac_x = 0.5 + 0.5 * jnp.tanh(displace[l][0])
                frac_y = 0.5 + 0.5 * jnp.tanh(displace[l][1])
            weight_x = [
                jnp.where(odd_x, frac_x, 1.0 - frac_x),
                jnp.where(odd_x, 1.0 - frac_x, frac_x),
            ]
            weight_y = [
                jnp.where(odd_y, frac_y, 1.0 - frac_y),
                jnp.where(odd_y, 1.0 - frac_y, frac_y),
            ]
            for c in range(n_comp):
                total = None
                for ry in range(2):
                    for rx in range(2):
                        term = weight_x[rx] * weight_y[ry] * taken[c * n_level + l, ry * 2 + rx]
                        total = term if total is None else total + term
                displace[l][c] = 0.5 * (mid[c * n_level + l].astype(jnp.float32) + total)
    for l in range(n_level):
        for c in range(n_comp):
            displace_ref[c, l] = displace[l][c]
    x0 = base_ref[ITERS, 0]
    y0 = base_ref[ITERS, 1]
    xs = [((x0 + ((r - x0) & 3)) >> 2) + r * 32 for r in range(4)]
    ys = [((y0 + ((r - y0) & 3)) >> 2) * 8 for r in range(4)]
    index = [(ys[ry] + xs[rx]).astype(jnp.int16) for ry in range(4) for rx in range(4)]
    for l in range(n_level):
        split = []
        for axis, start in ((0, x0), (1, y0)):
            w = lagrange_cubic(1.5 + 0.5 * jnp.tanh(displace[l][axis]))
            bit0 = (start & 1) == 1
            bit1 = (start & 2) == 2
            w = [jnp.where(bit0, w[(r - 1) & 3], w[r]) for r in range(4)]
            w = [jnp.where(bit1, w[(r - 2) & 3], w[r]) for r in range(4)]
            split.append(w)
        for ry in range(4):
            for rx in range(4):
                weight_ref[ry * 4 + rx, l] = split[0][rx] * split[1][ry]
        s = jnp.tanh(displace[l][2])
        layer_ref[l, 0] = 0.5 * s * (s - 1.0)
        layer_ref[l, 1] = 1.0 - s * s
        layer_ref[l, 2] = 0.5 * s * (s + 1.0)

    def one_tracer(t, carry):
        sums = {}
        for kind in range(16):
            at_lane = (kind // 4) * 128
            taken = []
            for e in range(n_ext):
                at = pl.multiple_of((t * n_ext + e) * nblocks, nblocks)
                values = patch_ref[pl.ds(at, nblocks), at_lane : at_lane + 128]
                taken.append(take_lanes(values, index[kind]))
            for l in range(n_level):
                weight = weight_ref[kind, l]
                for d in range(3):
                    term = weight * taken[l + d]
                    sums[l, d] = sums[l, d] + term if kind else term
        for l in range(n_level):
            total = layer_ref[l, 0] * sums[l, 0]
            total = total + layer_ref[l, 1] * sums[l, 1] + layer_ref[l, 2] * sums[l, 2]
            new_ref[t, l] = total.astype(jnp.bfloat16)
        return carry

    lax.fori_loop(0, n_tracer, one_tracer, 0)


def body(tracers, wind_field, regions, stencil_base, far_start):
    n_tracer, n_level, nblocks, cells = tracers.shape
    n_comp = wind_field.shape[0]
    n_bands = lax.axis_size("tile")
    below = shifted(tracers[:, n_level - 1], "lev", 1)
    above = shifted(tracers[:, 0], "lev", -1)
    packet = jnp.concatenate(
        [
            wind_field.reshape(-1, nblocks, cells),
            tracers.reshape(-1, nblocks, cells),
            below,
            above,
        ],
        axis=0,
    )
    lo2 = shifted(packet, "tile", 2)
    hi2 = shifted(packet, "tile", -2)
    cross = lax.ppermute(packet, "tile", [(i, ((i + 1) ^ 1) - 1) for i in range(1, n_bands - 1)])
    mate = lax.ppermute(packet, "tile", [(i, i ^ 1) for i in range(n_bands)])
    wind_rows = ITERS * n_comp * n_level * nblocks
    rows = n_tracer * (n_level + 2) * nblocks
    vmem = pl.BlockSpec(memory_space=pltpu.VMEM)
    return pl.pallas_call(
        transport_kernel,
        name="transport",
        out_shape=(
            jax.ShapeDtypeStruct(tracers.shape, jnp.bfloat16),
            jax.ShapeDtypeStruct(wind_field.shape, jnp.float32),
        ),
        in_specs=[vmem] * 8,
        out_specs=(vmem, vmem),
        scratch_shapes=[
            pltpu.VMEM((wind_rows, POINTS), jnp.bfloat16),
            pltpu.VMEM((wind_rows, POINTS), jnp.bfloat16),
            pltpu.VMEM((rows, POINTS), jnp.bfloat16),
            pltpu.VMEM((rows, POINTS), jnp.bfloat16),
            pltpu.VMEM((16, n_level, nblocks, cells), jnp.float32),
            pltpu.VMEM((n_level, 3, nblocks, cells), jnp.float32),
        ],
        compiler_params=pltpu.CompilerParams(vmem_limit_bytes=40 * 1024 * 1024),
    )(
        jnp.swapaxes(far_start, 1, 2),
        jnp.swapaxes(regions, 1, 2),
        stencil_base,
        mate,
        cross,
        hi2,
        lo2,
        packet,
    )


def solution(mesh):
    return jax.shard_map(
        body,
        mesh=mesh,
        in_specs=(
            P(None, "lev", "tile", None),
            P(None, "lev", "tile", None),
            P(None, "tile", None),
            P(None, None, "tile", None),
            P(),
        ),
        out_specs=(P(None, "lev", "tile", None), P(None, "lev", "tile", None)),
        check_vma=False,
    )
```

```python
import jax
import jax.numpy as jnp
from jax import lax
from jax.experimental import pallas as pl
from jax.experimental.pallas import tpu as pltpu
from jax.sharding import PartitionSpec as P

ITERS = 3
BW = 16
BH = 8
CELLS = BW * BH
QUADS = 4
POINTS = QUADS * CELLS
N_OFF = 5


def swapped(shard, axis, first, by):
    devices = lax.axis_size(axis)
    pairs = []
    for i in range(first, devices):
        j = ((i - first) ^ by) + first
        if j < devices:
            pairs.append((i, j))
    return lax.ppermute(shard, axis, pairs)


def lagrange_cubic(position):
    return [
        -(position - 1.0) * (position - 2.0) * (position - 3.0) / 6.0,
        position * (position - 2.0) * (position - 3.0) / 2.0,
        -position * (position - 1.0) * (position - 3.0) / 2.0,
        position * (position - 1.0) * (position - 2.0) / 6.0,
    ]


def column(row, count):
    at = lax.broadcasted_iota(jnp.int32, (count, count), 0)
    lane = lax.broadcasted_iota(jnp.int32, (count, count), 1)
    return jnp.sum(jnp.where(at == lane, row, 0), axis=1, keepdims=True)


def selectors(regions, starts, own_band, nblocks):
    upper = column(regions[0:1], nblocks)
    left = column(regions[1:2], nblocks)
    mate = jnp.where((own_band & 1) == 0, 1, -1)
    paired = jnp.where((own_band & 2) == 0, 2, -2)
    lane = lax.broadcasted_iota(jnp.int32, (nblocks, N_OFF * nblocks), 1)
    rows = []
    for quad_y in (0, 1):
        for quad_x in (0, 1):
            offset = upper + (quad_y - own_band)
            col = (left + quad_x) & (nblocks - 1)
            run_low = (col - starts[0]) & (nblocks - 1)
            run_high = (col - starts[1]) & (nblocks - 1)
            run = jnp.where(offset == -2, run_low, jnp.where(offset == 2, run_high, 0))
            place = jnp.where(offset == mate, 1, jnp.where(offset == -mate, 3, 2))
            place = jnp.where(offset == paired, 4, jnp.where(offset == -paired, 0, place))
            slot = jnp.where(run < nblocks // 2, place * nblocks + col, -1)
            rows.append(jnp.where(lane == slot, 1.0, 0.0).astype(jnp.bfloat16))
    return jnp.concatenate(rows, axis=0)


def run_starts(far, own_band):
    n_bands = far.shape[1]
    lane = lax.broadcasted_iota(jnp.int32, (1, n_bands), 1)
    picked = []
    for side, band in ((0, own_band - 2), (1, own_band + 2)):
        band = jnp.clip(band, 0, n_bands - 1)
        picked.append(
            jnp.sum(jnp.where(lane == band, far[side : side + 1], 0), axis=1, keepdims=True)
        )
    return picked


def class_order(log_step):
    step = 1 << log_step
    mask = step - 1
    source = lax.broadcasted_iota(jnp.int32, (POINTS, 128), 0)
    lane = lax.broadcasted_iota(jnp.int32, (POINTS, 128), 1)
    x = (source & (BW - 1)) + ((source >> 7) & 1) * BW
    y = ((source >> 4) & (BH - 1)) + (source >> 8) * BH
    kind = (y & mask) * step + (x & mask)
    place = (y >> log_step) * (2 * BW // step) + (x >> log_step)
    dest = kind * (POINTS // (step * step)) + place
    cols = [
        jnp.where(dest == lane + v * 128, 1.0, 0.0).astype(jnp.bfloat16) for v in range(QUADS)
    ]
    return jnp.concatenate(cols, axis=1)


def sort_rows(picked, nblocks, lanes_at):
    return jnp.concatenate(
        [
            picked[q * nblocks : (q + 1) * nblocks, lanes_at : lanes_at + CELLS]
            for q in range(QUADS)
        ],
        axis=1,
    )


LANES = lax.GatherDimensionNumbers(
    offset_dims=(),
    collapsed_slice_dims=(1,),
    start_index_map=(1,),
    operand_batching_dims=(0,),
    start_indices_batching_dims=(0,),
)


def take_lanes(values, index):
    picked = lax.gather(
        values,
        index[..., None],
        LANES,
        slice_sizes=(1, 1),
        mode=lax.GatherScatterMode.PROMISE_IN_BOUNDS,
    )
    return picked.astype(jnp.float32)


def transport_kernel(
    far_ref,
    regions_ref,
    base_ref,
    mate,
    cross,
    even2,
    odd2,
    mid,
    new_ref,
    displace_ref,
    wind_rows,
    wind_patch,
    rows_ref,
    patch_ref,
    weight_ref,
    layer_ref,
):
    n_tracer, n_level, nblocks, _ = new_ref.shape
    n_comp = displace_ref.shape[0]
    n_ext = n_level + 2
    own = lax.axis_index("tile")
    picks = [
        selectors(regions_ref[k], run_starts(far_ref[k], own), own, nblocks)
        for k in range(ITERS + 1)
    ]
    bands = (odd2, mate, mid, cross, even2)

    def stacked(row):
        return jnp.concatenate([b[row] for b in bands], axis=0)

    n_field = n_comp * n_level
    pick = jnp.concatenate(picks[:ITERS], axis=0)
    for i in range(0, n_field, 2):
        picked = jnp.dot(
            pick,
            jnp.concatenate([stacked(i), stacked(i + 1)], axis=1),
            preferred_element_type=jnp.float32,
        ).astype(jnp.bfloat16)
        for k in range(ITERS):
            part = picked[k * QUADS * nblocks : (k + 1) * QUADS * nblocks]
            for half in range(2):
                at = (k * n_field + i + half) * nblocks
                wind_rows[at : at + nblocks, :] = sort_rows(part, nblocks, half * CELLS)
    wind_patch[...] = jnp.dot(
        wind_rows[...], class_order(1), preferred_element_type=jnp.float32
    ).astype(jnp.bfloat16)
    for t in range(n_tracer):
        levels = [stacked(n_field + t * n_level + l) for l in range(n_level)]
        below = stacked(n_field + n_tracer * n_level + t)
        above = stacked(n_field + n_tracer * (n_level + 1) + t)
        levels = [below] + levels + [above]
        for e in range(0, n_ext, 2):
            picked = jnp.dot(
                picks[ITERS],
                jnp.concatenate(levels[e : e + 2], axis=1),
                preferred_element_type=jnp.float32,
            ).astype(jnp.bfloat16)
            for half in range(2):
                at = (t * n_ext + e + half) * nblocks
                rows_ref[at : at + nblocks, :] = sort_rows(picked, nblocks, half * CELLS)
    patch_ref[...] = jnp.dot(
        rows_ref[...], class_order(2), preferred_element_type=jnp.float32
    ).astype(jnp.bfloat16)
    displace = [[None] * n_comp for _ in range(n_level)]
    for k in range(ITERS):
        x0 = base_ref[k, 0] + 1
        y0 = base_ref[k, 1] + 1
        xs = [(x0 + 1) >> 1, x0 >> 1]
        ys = [((y0 + 1) >> 1) * BW, (y0 >> 1) * BW]
        index = [[(ys[ry] + xs[rx]).astype(jnp.int16) for rx in range(2)] for ry in range(2)]
        odd_x = (x0 & 1) == 1
        odd_y = (y0 & 1) == 1
        taken = {}
        for ry in range(2):
            for rx in range(2):
                kind = ry * 2 + rx
                for i in range(n_field):
                    at = (k * n_field + i) * nblocks
                    values = wind_patch[at : at + nblocks, kind * 128 : (kind + 1) * 128]
                    taken[i, kind] = take_lanes(values, index[ry][rx])
        for l in range(n_level):
            if k == 0:
                frac_x = jnp.full(x0.shape, 0.5, jnp.float32)
                frac_y = frac_x
            else:
                frac_x = 0.5 + 0.5 * jnp.tanh(displace[l][0])
                frac_y = 0.5 + 0.5 * jnp.tanh(displace[l][1])
            weight_x = [
                jnp.where(odd_x, frac_x, 1.0 - frac_x),
                jnp.where(odd_x, 1.0 - frac_x, frac_x),
            ]
            weight_y = [
                jnp.where(odd_y, frac_y, 1.0 - frac_y),
                jnp.where(odd_y, 1.0 - frac_y, frac_y),
            ]
            for c in range(n_comp):
                total = None
                for ry in range(2):
                    for rx in range(2):
                        term = weight_x[rx] * weight_y[ry] * taken[c * n_level + l, ry * 2 + rx]
                        total = term if total is None else total + term
                displace[l][c] = 0.5 * (mid[c * n_level + l].astype(jnp.float32) + total)
    for l in range(n_level):
        for c in range(n_comp):
            displace_ref[c, l] = displace[l][c]
    x0 = base_ref[ITERS, 0]
    y0 = base_ref[ITERS, 1]
    xs = [((x0 + ((r - x0) & 3)) >> 2) + r * 32 for r in range(4)]
    ys = [((y0 + ((r - y0) & 3)) >> 2) * 8 for r in range(4)]
    index = [(ys[ry] + xs[rx]).astype(jnp.int16) for ry in range(4) for rx in range(4)]
    for l in range(n_level):
        split = []
        for axis, start in ((0, x0), (1, y0)):
            w = lagrange_cubic(1.5 + 0.5 * jnp.tanh(displace[l][axis]))
            bit0 = (start & 1) == 1
            bit1 = (start & 2) == 2
            w = [jnp.where(bit0, w[(r - 1) & 3], w[r]) for r in range(4)]
            w = [jnp.where(bit1, w[(r - 2) & 3], w[r]) for r in range(4)]
            split.append(w)
        for ry in range(4):
            for rx in range(4):
                weight_ref[ry * 4 + rx, l] = split[0][rx] * split[1][ry]
        s = jnp.tanh(displace[l][2])
        layer_ref[l, 0] = 0.5 * s * (s - 1.0)
        layer_ref[l, 1] = 1.0 - s * s
        layer_ref[l, 2] = 0.5 * s * (s + 1.0)

    def one_tracer(t, carry):
        sums = {}
        for kind in range(16):
            at_lane = (kind // 4) * 128
            taken = []
            for e in range(n_ext):
                at = pl.multiple_of((t * n_ext + e) * nblocks, nblocks)
                values = patch_ref[pl.ds(at, nblocks), at_lane : at_lane + 128]
                taken.append(take_lanes(values, index[kind]))
            for l in range(n_level):
                weight = weight_ref[kind, l]
                for d in range(3):
                    term = weight * taken[l + d]
                    sums[l, d] = sums[l, d] + term if kind else term
        for l in range(n_level):
            total = layer_ref[l, 0] * sums[l, 0]
            total = total + layer_ref[l, 1] * sums[l, 1] + layer_ref[l, 2] * sums[l, 2]
            new_ref[t, l] = total.astype(jnp.bfloat16)
        return carry

    lax.fori_loop(0, n_tracer, one_tracer, 0)


def body(tracers, wind_field, regions, stencil_base, far_start):
    n_tracer, n_level, nblocks, cells = tracers.shape
    n_comp = wind_field.shape[0]
    level_pos = lax.axis_index("lev")
    even = level_pos % 2 == 0
    bottom, top = tracers[:, 0], tracers[:, n_level - 1]
    got_odd = swapped(jnp.where(even, bottom, top), "lev", 1, 1)
    got_even = swapped(jnp.where(even, top, bottom), "lev", 0, 1)
    below = jnp.where(even, got_odd, got_even)
    above = jnp.where(even, got_even, got_odd)
    packet = jnp.concatenate(
        [
            wind_field.reshape(-1, nblocks, cells),
            tracers.reshape(-1, nblocks, cells),
            jnp.where(level_pos == 0, bottom, below),
            jnp.where(level_pos == lax.axis_size("lev") - 1, top, above),
        ],
        axis=0,
    )
    odd2 = swapped(packet, "tile", 2, 2)
    even2 = swapped(packet, "tile", 0, 2)
    cross = swapped(packet, "tile", 1, 1)
    mate = swapped(packet, "tile", 0, 1)
    wind_rows = ITERS * n_comp * n_level * nblocks
    rows = n_tracer * (n_level + 2) * nblocks
    vmem = pl.BlockSpec(memory_space=pltpu.VMEM)
    return pl.pallas_call(
        transport_kernel,
        name="transport",
        out_shape=(
            jax.ShapeDtypeStruct(tracers.shape, jnp.bfloat16),
            jax.ShapeDtypeStruct(wind_field.shape, jnp.float32),
        ),
        in_specs=[vmem] * 8,
        out_specs=(vmem, vmem),
        scratch_shapes=[
            pltpu.VMEM((wind_rows, POINTS), jnp.bfloat16),
            pltpu.VMEM((wind_rows, POINTS), jnp.bfloat16),
            pltpu.VMEM((rows, POINTS), jnp.bfloat16),
            pltpu.VMEM((rows, POINTS), jnp.bfloat16),
            pltpu.VMEM((16, n_level, nblocks, cells), jnp.float32),
            pltpu.VMEM((n_level, 3, nblocks, cells), jnp.float32),
        ],
        compiler_params=pltpu.CompilerParams(vmem_limit_bytes=40 * 1024 * 1024),
    )(
        jnp.swapaxes(far_start, 1, 2),
        jnp.swapaxes(regions, 1, 2),
        stencil_base,
        mate,
        cross,
        even2,
        odd2,
        packet,
    )


def solution(mesh):
    return jax.shard_map(
        body,
        mesh=mesh,
        in_specs=(
            P(None, "lev", "tile", None),
            P(None, "lev", "tile", None),
            P(None, "tile", None),
            P(None, None, "tile", None),
            P(),
        ),
        out_specs=(P(None, "lev", "tile", None), P(None, "lev", "tile", None)),
        check_vma=False,
    )
```

```python
import jax
import jax.numpy as jnp
from jax import lax
from jax.experimental import pallas as pl
from jax.experimental.pallas import tpu as pltpu
from jax.sharding import PartitionSpec as P

ITERS = 3
BW = 16
BH = 8
CELLS = BW * BH
QUADS = 4
POINTS = QUADS * CELLS
N_OFF = 6


def swapped(shard, axis, first, by):
    devices = lax.axis_size(axis)
    pairs = []
    for i in range(first, devices):
        j = ((i - first) ^ by) + first
        if j < devices:
            pairs.append((i, j))
    return lax.ppermute(shard, axis, pairs)


def lagrange_cubic(position):
    return [
        -(position - 1.0) * (position - 2.0) * (position - 3.0) / 6.0,
        position * (position - 2.0) * (position - 3.0) / 2.0,
        -position * (position - 1.0) * (position - 3.0) / 2.0,
        position * (position - 1.0) * (position - 2.0) / 6.0,
    ]


def column(row, count):
    at = lax.broadcasted_iota(jnp.int32, (count, count), 0)
    lane = lax.broadcasted_iota(jnp.int32, (count, count), 1)
    return jnp.sum(jnp.where(at == lane, row, 0), axis=1, keepdims=True)


def selectors(regions, starts, own_band, nblocks):
    upper = column(regions[0:1], nblocks)
    left = column(regions[1:2], nblocks)
    mate = jnp.where((own_band & 1) == 0, 1, -1)
    paired = jnp.where((own_band & 2) == 0, 2, -2)
    next_place = jnp.where(-2 * mate == paired, 3, 5)
    lane = lax.broadcasted_iota(jnp.int32, (nblocks, N_OFF * nblocks), 1)
    rows = []
    for quad_y in (0, 1):
        for quad_x in (0, 1):
            offset = upper + (quad_y - own_band)
            col = (left + quad_x) & (nblocks - 1)
            run_low = (col - starts[0]) & (nblocks - 1)
            run_high = (col - starts[1]) & (nblocks - 1)
            run = jnp.where(offset == -2, run_low, jnp.where(offset == 2, run_high, 0))
            place = jnp.where(offset == mate, 1, jnp.where(offset == -mate, next_place, 2))
            place = jnp.where(offset == paired, 4, jnp.where(offset == -paired, 0, place))
            slot = jnp.where(run < nblocks // 2, place * nblocks + col, -1)
            rows.append(jnp.where(lane == slot, 1.0, 0.0).astype(jnp.bfloat16))
    return jnp.concatenate(rows, axis=0)


def run_starts(far, own_band):
    n_bands = far.shape[1]
    lane = lax.broadcasted_iota(jnp.int32, (1, n_bands), 1)
    picked = []
    for side, band in ((0, own_band - 2), (1, own_band + 2)):
        band = jnp.clip(band, 0, n_bands - 1)
        picked.append(
            jnp.sum(jnp.where(lane == band, far[side : side + 1], 0), axis=1, keepdims=True)
        )
    return picked


def class_order(log_step, zero):
    step = 1 << log_step
    mask = step - 1
    source = lax.broadcasted_iota(jnp.int32, (POINTS, POINTS), 0) + zero
    lane = lax.broadcasted_iota(jnp.int32, (POINTS, POINTS), 1)
    x = (source & (BW - 1)) + ((source >> 7) & 1) * BW
    y = ((source >> 4) & (BH - 1)) + (source >> 8) * BH
    kind = (y & mask) * step + (x & mask)
    place = (y >> log_step) * (2 * BW // step) + (x >> log_step)
    return (kind * (POINTS // (step * step)) + place == lane).astype(jnp.bfloat16)


def sort_rows(picked, nblocks, lanes_at):
    return jnp.concatenate(
        [
            picked[q * nblocks : (q + 1) * nblocks, lanes_at : lanes_at + CELLS]
            for q in range(QUADS)
        ],
        axis=1,
    )


LANES = lax.GatherDimensionNumbers(
    offset_dims=(),
    collapsed_slice_dims=(1,),
    start_index_map=(1,),
    operand_batching_dims=(0,),
    start_indices_batching_dims=(0,),
)


def take_lanes(values, index):
    picked = lax.gather(
        values,
        index[..., None],
        LANES,
        slice_sizes=(1, 1),
        mode=lax.GatherScatterMode.PROMISE_IN_BOUNDS,
    )
    return picked.astype(jnp.float32)


def transport_kernel(
    far_ref,
    regions_ref,
    base_ref,
    order1_ref,
    order2_ref,
    mate,
    cross,
    even2,
    relay,
    odd2,
    mid,
    new_ref,
    displace_ref,
    wind_rows,
    wind_patch,
    rows_ref,
    patch_ref,
    weight_ref,
    layer_ref,
):
    n_tracer, n_level, nblocks, _ = new_ref.shape
    n_comp = displace_ref.shape[0]
    n_ext = n_level + 2
    own = lax.axis_index("tile")
    picks = [
        selectors(regions_ref[k], run_starts(far_ref[k], own), own, nblocks)
        for k in range(ITERS + 1)
    ]
    bands = (odd2, mate, mid, cross, even2, relay)

    def stacked(row):
        return jnp.concatenate([b[row] for b in bands], axis=0)

    n_field = n_comp * n_level
    pick = jnp.concatenate(picks[:ITERS], axis=0)
    for i in range(0, n_field, 2):
        picked = jnp.dot(
            pick,
            jnp.concatenate([stacked(i), stacked(i + 1)], axis=1),
            preferred_element_type=jnp.float32,
        ).astype(jnp.bfloat16)
        for k in range(ITERS):
            part = picked[k * QUADS * nblocks : (k + 1) * QUADS * nblocks]
            for half in range(2):
                at = (k * n_field + i + half) * nblocks
                wind_rows[at : at + nblocks, :] = sort_rows(part, nblocks, half * CELLS)
    wind_patch[...] = jnp.dot(
        wind_rows[...], order1_ref[...], preferred_element_type=jnp.float32
    ).astype(jnp.bfloat16)
    for t in range(n_tracer):
        levels = [stacked(n_field + t * n_level + l) for l in range(n_level)]
        below = stacked(n_field + n_tracer * n_level + t)
        above = stacked(n_field + n_tracer * (n_level + 1) + t)
        levels = [below] + levels + [above]
        for e in range(0, n_ext, 2):
            picked = jnp.dot(
                picks[ITERS],
                jnp.concatenate(levels[e : e + 2], axis=1),
                preferred_element_type=jnp.float32,
            ).astype(jnp.bfloat16)
            for half in range(2):
                at = (t * n_ext + e + half) * nblocks
                rows_ref[at : at + nblocks, :] = sort_rows(picked, nblocks, half * CELLS)
    patch_ref[...] = jnp.dot(
        rows_ref[...], order2_ref[...], preferred_element_type=jnp.float32
    ).astype(jnp.bfloat16)
    displace = [[None] * n_comp for _ in range(n_level)]
    for k in range(ITERS):
        x0 = base_ref[k, 0] + 1
        y0 = base_ref[k, 1] + 1
        xs = [(x0 + 1) >> 1, x0 >> 1]
        ys = [((y0 + 1) >> 1) * BW, (y0 >> 1) * BW]
        index = [[(ys[ry] + xs[rx]).astype(jnp.int16) for rx in range(2)] for ry in range(2)]
        odd_x = (x0 & 1) == 1
        odd_y = (y0 & 1) == 1
        taken = {}
        for ry in range(2):
            for rx in range(2):
                kind = ry * 2 + rx
                for i in range(n_field):
                    at = (k * n_field + i) * nblocks
                    values = wind_patch[at : at + nblocks, kind * 128 : (kind + 1) * 128]
                    taken[i, kind] = take_lanes(values, index[ry][rx])
        for l in range(n_level):
            if k == 0:
                frac_x = jnp.full(x0.shape, 0.5, jnp.float32)
                frac_y = frac_x
            else:
                frac_x = 0.5 + 0.5 * jnp.tanh(displace[l][0])
                frac_y = 0.5 + 0.5 * jnp.tanh(displace[l][1])
            weight_x = [
                jnp.where(odd_x, frac_x, 1.0 - frac_x),
                jnp.where(odd_x, 1.0 - frac_x, frac_x),
            ]
            weight_y = [
                jnp.where(odd_y, frac_y, 1.0 - frac_y),
                jnp.where(odd_y, 1.0 - frac_y, frac_y),
            ]
            for c in range(n_comp):
                total = None
                for ry in range(2):
                    for rx in range(2):
                        term = weight_x[rx] * weight_y[ry] * taken[c * n_level + l, ry * 2 + rx]
                        total = term if total is None else total + term
                displace[l][c] = 0.5 * (mid[c * n_level + l].astype(jnp.float32) + total)
    for l in range(n_level):
        for c in range(n_comp):
            displace_ref[c, l] = displace[l][c]
    x0 = base_ref[ITERS, 0]
    y0 = base_ref[ITERS, 1]
    xs = [((x0 + ((r - x0) & 3)) >> 2) + r * 32 for r in range(4)]
    ys = [((y0 + ((r - y0) & 3)) >> 2) * 8 for r in range(4)]
    index = [(ys[ry] + xs[rx]).astype(jnp.int16) for ry in range(4) for rx in range(4)]
    for l in range(n_level):
        split = []
        for axis, start in ((0, x0), (1, y0)):
            w = lagrange_cubic(1.5 + 0.5 * jnp.tanh(displace[l][axis]))
            bit0 = (start & 1) == 1
            bit1 = (start & 2) == 2
            w = [jnp.where(bit0, w[(r - 1) & 3], w[r]) for r in range(4)]
            w = [jnp.where(bit1, w[(r - 2) & 3], w[r]) for r in range(4)]
            split.append(w)
        for ry in range(4):
            for rx in range(4):
                weight_ref[ry * 4 + rx, l] = split[0][rx] * split[1][ry]
        s = jnp.tanh(displace[l][2])
        layer_ref[l, 0] = 0.5 * s * (s - 1.0)
        layer_ref[l, 1] = 1.0 - s * s
        layer_ref[l, 2] = 0.5 * s * (s + 1.0)

    def one_tracer(t, carry):
        sums = {}
        for kind in range(16):
            at_lane = (kind // 4) * 128
            taken = []
            for e in range(n_ext):
                at = pl.multiple_of((t * n_ext + e) * nblocks, nblocks)
                values = patch_ref[pl.ds(at, nblocks), at_lane : at_lane + 128]
                taken.append(take_lanes(values, index[kind]))
            for l in range(n_level):
                weight = weight_ref[kind, l]
                for d in range(3):
                    term = weight * taken[l + d]
                    sums[l, d] = sums[l, d] + term if kind else term
        for l in range(n_level):
            total = layer_ref[l, 0] * sums[l, 0]
            total = total + layer_ref[l, 1] * sums[l, 1] + layer_ref[l, 2] * sums[l, 2]
            new_ref[t, l] = total.astype(jnp.bfloat16)
        return carry

    lax.fori_loop(0, n_tracer, one_tracer, 0, unroll=4)


def body(tracers, wind_field, regions, stencil_base, far_start):
    n_tracer, n_level, nblocks, cells = tracers.shape
    n_comp = wind_field.shape[0]
    level_pos = lax.axis_index("lev")
    even = level_pos % 2 == 0
    bottom, top = tracers[:, 0], tracers[:, n_level - 1]
    got_odd = swapped(jnp.where(even, bottom, top), "lev", 1, 1)
    got_even = swapped(jnp.where(even, top, bottom), "lev", 0, 1)
    below = jnp.where(even, got_odd, got_even)
    above = jnp.where(even, got_even, got_odd)
    packet = jnp.concatenate(
        [
            wind_field.reshape(-1, nblocks, cells),
            tracers.reshape(-1, nblocks, cells),
            jnp.where(level_pos == 0, bottom, below),
            jnp.where(level_pos == lax.axis_size("lev") - 1, top, above),
        ],
        axis=0,
    )
    odd2 = swapped(packet, "tile", 2, 2)
    even2 = swapped(packet, "tile", 0, 2)
    n_bands = lax.axis_size("tile")
    pairs = [(i, i ^ 3) for i in range(n_bands) if i % 4 in (1, 2)]
    cross = lax.ppermute(packet, "tile", pairs)
    pairs = [(i, i ^ 1) for i in range(2, n_bands - 2) if i % 4 in (1, 2)]
    relay = lax.ppermute(odd2, "tile", pairs)
    mate = swapped(packet, "tile", 0, 1)
    _, zero = lax.optimization_barrier((packet[0, 0], jnp.int32(0)))
    wind_rows = ITERS * n_comp * n_level * nblocks
    rows = n_tracer * (n_level + 2) * nblocks
    vmem = pl.BlockSpec(memory_space=pltpu.VMEM)
    return pl.pallas_call(
        transport_kernel,
        name="transport",
        out_shape=(
            jax.ShapeDtypeStruct(tracers.shape, jnp.bfloat16),
            jax.ShapeDtypeStruct(wind_field.shape, jnp.float32),
        ),
        in_specs=[vmem] * 11,
        out_specs=(vmem, vmem),
        scratch_shapes=[
            pltpu.VMEM((wind_rows, POINTS), jnp.bfloat16),
            pltpu.VMEM((wind_rows, POINTS), jnp.bfloat16),
            pltpu.VMEM((rows, POINTS), jnp.bfloat16),
            pltpu.VMEM((rows, POINTS), jnp.bfloat16),
            pltpu.VMEM((16, n_level, nblocks, cells), jnp.float32),
            pltpu.VMEM((n_level, 3, nblocks, cells), jnp.float32),
        ],
        compiler_params=pltpu.CompilerParams(vmem_limit_bytes=16 * 1024 * 1024),
    )(
        jnp.swapaxes(far_start, 1, 2),
        jnp.swapaxes(regions, 1, 2),
        stencil_base,
        class_order(1, zero),
        class_order(2, zero),
        mate,
        cross,
        even2,
        relay,
        odd2,
        packet,
    )


def solution(mesh):
    return jax.shard_map(
        body,
        mesh=mesh,
        in_specs=(
            P(None, "lev", "tile", None),
            P(None, "lev", "tile", None),
            P(None, "tile", None),
            P(None, None, "tile", None),
            P(),
        ),
        out_specs=(P(None, "lev", "tile", None), P(None, "lev", "tile", None)),
        check_vma=False,
    )
```

```python
import jax
import jax.numpy as jnp
from jax import lax
from jax.experimental import pallas as pl
from jax.experimental.pallas import tpu as pltpu
from jax.sharding import PartitionSpec as P

ITERS = 3
BW = 16
BH = 8
CELLS = BW * BH
QUADS = 4
POINTS = QUADS * CELLS
N_OFF = 6


def swapped(shard, axis, first, by):
    devices = lax.axis_size(axis)
    pairs = []
    for i in range(first, devices):
        j = ((i - first) ^ by) + first
        if j < devices:
            pairs.append((i, j))
    return lax.ppermute(shard, axis, pairs)


def lagrange_cubic(position):
    return [
        -(position - 1.0) * (position - 2.0) * (position - 3.0) / 6.0,
        position * (position - 2.0) * (position - 3.0) / 2.0,
        -position * (position - 1.0) * (position - 3.0) / 2.0,
        position * (position - 1.0) * (position - 2.0) / 6.0,
    ]


def column(row, count):
    at = lax.broadcasted_iota(jnp.int32, (count, count), 0)
    lane = lax.broadcasted_iota(jnp.int32, (count, count), 1)
    return jnp.sum(jnp.where(at == lane, row, 0), axis=1, keepdims=True)


def selectors(regions, starts, own_band, nblocks):
    upper = column(regions[0:1], nblocks)
    left = column(regions[1:2], nblocks)
    mate = jnp.where((own_band & 1) == 0, 1, -1)
    paired = jnp.where((own_band & 2) == 0, 2, -2)
    next_place = jnp.where(-2 * mate == paired, 3, 5)
    lane = lax.broadcasted_iota(jnp.int32, (nblocks, N_OFF * nblocks), 1)
    rows = []
    for quad_y in (0, 1):
        for quad_x in (0, 1):
            offset = upper + (quad_y - own_band)
            col = (left + quad_x) & (nblocks - 1)
            run_low = (col - starts[0]) & (nblocks - 1)
            run_high = (col - starts[1]) & (nblocks - 1)
            run = jnp.where(offset == -2, run_low, jnp.where(offset == 2, run_high, 0))
            place = jnp.where(offset == mate, 1, jnp.where(offset == -mate, next_place, 2))
            place = jnp.where(offset == paired, 4, jnp.where(offset == -paired, 0, place))
            slot = jnp.where(run < nblocks // 2, place * nblocks + col, -1)
            rows.append(jnp.where(lane == slot, 1.0, 0.0).astype(jnp.bfloat16))
    return jnp.concatenate(rows, axis=0)


def run_starts(far, own_band):
    n_bands = far.shape[1]
    lane = lax.broadcasted_iota(jnp.int32, (1, n_bands), 1)
    picked = []
    for side, band in ((0, own_band - 2), (1, own_band + 2)):
        band = jnp.clip(band, 0, n_bands - 1)
        picked.append(
            jnp.sum(jnp.where(lane == band, far[side : side + 1], 0), axis=1, keepdims=True)
        )
    return picked


def class_order(log_step, zero):
    step = 1 << log_step
    mask = step - 1
    source = lax.broadcasted_iota(jnp.int32, (POINTS, POINTS), 0) + zero
    lane = lax.broadcasted_iota(jnp.int32, (POINTS, POINTS), 1)
    x = (source & (BW - 1)) + ((source >> 7) & 1) * BW
    y = ((source >> 4) & (BH - 1)) + (source >> 8) * BH
    kind = (y & mask) * step + (x & mask)
    place = (y >> log_step) * (2 * BW // step) + (x >> log_step)
    return (kind * (POINTS // (step * step)) + place == lane).astype(jnp.bfloat16)


def sort_rows(picked, nblocks, lanes_at):
    return jnp.concatenate(
        [
            picked[q * nblocks : (q + 1) * nblocks, lanes_at : lanes_at + CELLS]
            for q in range(QUADS)
        ],
        axis=1,
    )


LANES = lax.GatherDimensionNumbers(
    offset_dims=(),
    collapsed_slice_dims=(1,),
    start_index_map=(1,),
    operand_batching_dims=(0,),
    start_indices_batching_dims=(0,),
)


def take_lanes(values, index):
    picked = lax.gather(
        values,
        index[..., None],
        LANES,
        slice_sizes=(1, 1),
        mode=lax.GatherScatterMode.PROMISE_IN_BOUNDS,
    )
    return picked.astype(jnp.float32)


def transport_kernel(
    far_ref,
    regions_ref,
    base_ref,
    order1_ref,
    order2_ref,
    mate,
    cross,
    even2,
    relay,
    odd2,
    mid,
    new_ref,
    displace_ref,
    wind_rows,
    wind_patch,
    rows_ref,
    patch_ref,
    weight_ref,
    layer_ref,
):
    n_tracer, n_level, nblocks, _ = new_ref.shape
    n_comp = displace_ref.shape[0]
    n_ext = n_level + 2
    own = lax.axis_index("tile")
    picks = [
        selectors(regions_ref[k], run_starts(far_ref[k], own), own, nblocks)
        for k in range(ITERS + 1)
    ]
    bands = (odd2, mate, mid, cross, even2, relay)

    def stacked(row):
        return jnp.concatenate([b[row] for b in bands], axis=0)

    n_field = n_comp * n_level
    pick = jnp.concatenate(picks[:ITERS], axis=0)
    for i in range(0, n_field, 2):
        picked = jnp.dot(
            pick,
            jnp.concatenate([stacked(i), stacked(i + 1)], axis=1),
            preferred_element_type=jnp.float32,
        ).astype(jnp.bfloat16)
        for k in range(ITERS):
            part = picked[k * QUADS * nblocks : (k + 1) * QUADS * nblocks]
            for half in range(2):
                at = (k * n_field + i + half) * nblocks
                wind_rows[at : at + nblocks, :] = sort_rows(part, nblocks, half * CELLS)
    wind_patch[...] = jnp.dot(
        wind_rows[...], order1_ref[...], preferred_element_type=jnp.float32
    ).astype(jnp.bfloat16)
    for t in range(n_tracer):
        levels = [stacked(n_field + t * n_level + l) for l in range(n_level)]
        below = stacked(n_field + n_tracer * n_level + t)
        above = stacked(n_field + n_tracer * (n_level + 1) + t)
        levels = [below] + levels + [above]
        for e in range(0, n_ext, 2):
            picked = jnp.dot(
                picks[ITERS],
                jnp.concatenate(levels[e : e + 2], axis=1),
                preferred_element_type=jnp.float32,
            ).astype(jnp.bfloat16)
            for half in range(2):
                at = (t * n_ext + e + half) * nblocks
                rows_ref[at : at + nblocks, :] = sort_rows(picked, nblocks, half * CELLS)
    patch_ref[...] = jnp.dot(
        rows_ref[...], order2_ref[...], preferred_element_type=jnp.float32
    ).astype(jnp.bfloat16)
    displace = [[None] * n_comp for _ in range(n_level)]
    for k in range(ITERS):
        x0 = base_ref[k, 0] + 1
        y0 = base_ref[k, 1] + 1
        xs = [(x0 + 1) >> 1, x0 >> 1]
        ys = [((y0 + 1) >> 1) * BW, (y0 >> 1) * BW]
        index = [[(ys[ry] + xs[rx]).astype(jnp.int16) for rx in range(2)] for ry in range(2)]
        odd_x = (x0 & 1) == 1
        odd_y = (y0 & 1) == 1
        taken = {}
        for ry in range(2):
            for rx in range(2):
                kind = ry * 2 + rx
                for i in range(n_field):
                    at = (k * n_field + i) * nblocks
                    values = wind_patch[at : at + nblocks, kind * 128 : (kind + 1) * 128]
                    taken[i, kind] = take_lanes(values, index[ry][rx])
        for l in range(n_level):
            if k == 0:
                frac_x = jnp.full(x0.shape, 0.5, jnp.float32)
                frac_y = frac_x
            else:
                frac_x = 0.5 + 0.5 * jnp.tanh(displace[l][0])
                frac_y = 0.5 + 0.5 * jnp.tanh(displace[l][1])
            weight_x = [
                jnp.where(odd_x, frac_x, 1.0 - frac_x),
                jnp.where(odd_x, 1.0 - frac_x, frac_x),
            ]
            weight_y = [
                jnp.where(odd_y, frac_y, 1.0 - frac_y),
                jnp.where(odd_y, 1.0 - frac_y, frac_y),
            ]
            for c in range(n_comp):
                total = None
                for ry in range(2):
                    for rx in range(2):
                        term = weight_x[rx] * weight_y[ry] * taken[c * n_level + l, ry * 2 + rx]
                        total = term if total is None else total + term
                displace[l][c] = 0.5 * (mid[c * n_level + l].astype(jnp.float32) + total)
    for l in range(n_level):
        for c in range(n_comp):
            displace_ref[c, l] = displace[l][c]
    x0 = base_ref[ITERS, 0]
    y0 = base_ref[ITERS, 1]
    xs = [((x0 + ((r - x0) & 3)) >> 2) + r * 32 for r in range(4)]
    ys = [((y0 + ((r - y0) & 3)) >> 2) * 8 for r in range(4)]
    index = [(ys[ry] + xs[rx]).astype(jnp.int16) for ry in range(4) for rx in range(4)]
    for l in range(n_level):
        split = []
        for axis, start in ((0, x0), (1, y0)):
            w = lagrange_cubic(1.5 + 0.5 * jnp.tanh(displace[l][axis]))
            bit0 = (start & 1) == 1
            bit1 = (start & 2) == 2
            w = [jnp.where(bit0, w[(r - 1) & 3], w[r]) for r in range(4)]
            w = [jnp.where(bit1, w[(r - 2) & 3], w[r]) for r in range(4)]
            split.append(w)
        for ry in range(4):
            for rx in range(4):
                weight_ref[ry * 4 + rx, l] = split[0][rx] * split[1][ry]
        s = jnp.tanh(displace[l][2])
        layer_ref[l, 0] = 0.5 * s * (s - 1.0)
        layer_ref[l, 1] = 1.0 - s * s
        layer_ref[l, 2] = 0.5 * s * (s + 1.0)

    def one_tracer(t, carry):
        sums = {}
        for kind in range(16):
            at_lane = (kind // 4) * 128
            taken = []
            for e in range(n_ext):
                at = pl.multiple_of((t * n_ext + e) * nblocks, nblocks)
                values = patch_ref[pl.ds(at, nblocks), at_lane : at_lane + 128]
                taken.append(take_lanes(values, index[kind]))
            for l in range(n_level):
                weight = weight_ref[kind, l]
                for d in range(3):
                    term = weight * taken[l + d]
                    sums[l, d] = sums[l, d] + term if kind else term
        for l in range(n_level):
            total = layer_ref[l, 0] * sums[l, 0]
            total = total + layer_ref[l, 1] * sums[l, 1] + layer_ref[l, 2] * sums[l, 2]
            new_ref[t, l] = total.astype(jnp.bfloat16)
        return carry

    lax.fori_loop(0, n_tracer, one_tracer, 0, unroll=4)


def body(tracers, wind_field, regions, stencil_base, far_start):
    n_tracer, n_level, nblocks, cells = tracers.shape
    n_comp = wind_field.shape[0]
    level_pos = lax.axis_index("lev")
    even = level_pos % 2 == 0
    bottom, top = tracers[:, 0], tracers[:, n_level - 1]
    got_odd = swapped(jnp.where(even, bottom, top), "lev", 1, 1)
    got_even = swapped(jnp.where(even, top, bottom), "lev", 0, 1)
    odd = level_pos % 2 == 1
    below = jnp.where(odd, got_even, got_odd)
    above = jnp.where(odd, got_odd, got_even)
    packet = jnp.concatenate(
        [
            wind_field.reshape(-1, nblocks, cells),
            tracers.reshape(-1, nblocks, cells),
            jnp.where(level_pos == 0, bottom, below),
            jnp.where(level_pos == lax.axis_size("lev") - 1, top, above),
        ],
        axis=0,
    )
    odd2 = swapped(packet, "tile", 2, 2)
    even2 = swapped(packet, "tile", 0, 2)
    n_bands = lax.axis_size("tile")
    pairs = [(i, i ^ 3) for i in range(n_bands) if i % 4 in (1, 2)]
    cross = lax.ppermute(packet, "tile", pairs)
    pairs = [(i, i ^ 1) for i in range(2, n_bands - 2) if i % 4 in (1, 2)]
    relay = lax.ppermute(odd2, "tile", pairs)
    mate = swapped(packet, "tile", 0, 1)
    _, zero = lax.optimization_barrier((packet[0, 0], jnp.int32(0)))
    wind_rows = ITERS * n_comp * n_level * nblocks
    rows = n_tracer * (n_level + 2) * nblocks
    vmem = pl.BlockSpec(memory_space=pltpu.VMEM)
    return pl.pallas_call(
        transport_kernel,
        name="transport",
        out_shape=(
            jax.ShapeDtypeStruct(tracers.shape, jnp.bfloat16),
            jax.ShapeDtypeStruct(wind_field.shape, jnp.float32),
        ),
        in_specs=[vmem] * 11,
        out_specs=(vmem, vmem),
        scratch_shapes=[
            pltpu.VMEM((wind_rows, POINTS), jnp.bfloat16),
            pltpu.VMEM((wind_rows, POINTS), jnp.bfloat16),
            pltpu.VMEM((rows, POINTS), jnp.bfloat16),
            pltpu.VMEM((rows, POINTS), jnp.bfloat16),
            pltpu.VMEM((16, n_level, nblocks, cells), jnp.float32),
            pltpu.VMEM((n_level, 3, nblocks, cells), jnp.float32),
        ],
        compiler_params=pltpu.CompilerParams(vmem_limit_bytes=16 * 1024 * 1024),
    )(
        jnp.swapaxes(far_start, 1, 2),
        jnp.swapaxes(regions, 1, 2),
        stencil_base,
        class_order(1, zero),
        class_order(2, zero),
        mate,
        cross,
        even2,
        relay,
        odd2,
        packet,
    )


def solution(mesh):
    return jax.shard_map(
        body,
        mesh=mesh,
        in_specs=(
            P(None, "lev", "tile", None),
            P(None, "lev", "tile", None),
            P(None, "tile", None),
            P(None, None, "tile", None),
            P(),
        ),
        out_specs=(P(None, "lev", "tile", None), P(None, "lev", "tile", None)),
        check_vma=False,
    )
```

```python
import jax
import jax.numpy as jnp
from jax import lax
from jax.experimental import pallas as pl
from jax.experimental.pallas import tpu as pltpu
from jax.sharding import PartitionSpec as P

ITERS = 3
BW = 16
BH = 8
CELLS = BW * BH
QUADS = 4
POINTS = QUADS * CELLS
N_OFF = 6


def swapped(shard, axis, first, by):
    devices = lax.axis_size(axis)
    pairs = []
    for i in range(first, devices):
        j = ((i - first) ^ by) + first
        if j < devices:
            pairs.append((i, j))
    return lax.ppermute(shard, axis, pairs)


def lagrange_cubic(position):
    return [
        -(position - 1.0) * (position - 2.0) * (position - 3.0) / 6.0,
        position * (position - 2.0) * (position - 3.0) / 2.0,
        -position * (position - 1.0) * (position - 3.0) / 2.0,
        position * (position - 1.0) * (position - 2.0) / 6.0,
    ]


def column(row, count):
    at = lax.broadcasted_iota(jnp.int32, (count, count), 0)
    lane = lax.broadcasted_iota(jnp.int32, (count, count), 1)
    return jnp.sum(jnp.where(at == lane, row, 0), axis=1, keepdims=True)


def selectors(regions, starts, own_band, nblocks):
    upper = column(regions[0:1], nblocks)
    left = column(regions[1:2], nblocks)
    mate = jnp.where((own_band & 1) == 0, 1, -1)
    paired = jnp.where((own_band & 2) == 0, 2, -2)
    next_place = jnp.where(-2 * mate == paired, 3, 5)
    lane = lax.broadcasted_iota(jnp.int32, (nblocks, N_OFF * nblocks), 1)
    rows = []
    for quad_y in (0, 1):
        for quad_x in (0, 1):
            offset = upper + (quad_y - own_band)
            col = (left + quad_x) & (nblocks - 1)
            run_low = (col - starts[0]) & (nblocks - 1)
            run_high = (col - starts[1]) & (nblocks - 1)
            run = jnp.where(offset == -2, run_low, jnp.where(offset == 2, run_high, 0))
            place = jnp.where(offset == mate, 1, jnp.where(offset == -mate, next_place, 2))
            place = jnp.where(offset == paired, 4, jnp.where(offset == -paired, 0, place))
            slot = jnp.where(run < nblocks // 2, place * nblocks + col, -1)
            rows.append(jnp.where(lane == slot, 1.0, 0.0).astype(jnp.bfloat16))
    return jnp.concatenate(rows, axis=0)


def run_starts(far, own_band):
    n_bands = far.shape[1]
    lane = lax.broadcasted_iota(jnp.int32, (1, n_bands), 1)
    picked = []
    for side, band in ((0, own_band - 2), (1, own_band + 2)):
        band = jnp.clip(band, 0, n_bands - 1)
        picked.append(
            jnp.sum(jnp.where(lane == band, far[side : side + 1], 0), axis=1, keepdims=True)
        )
    return picked


def class_order(log_step, zero):
    step = 1 << log_step
    mask = step - 1
    source = lax.broadcasted_iota(jnp.int32, (POINTS, POINTS), 0) + zero
    lane = lax.broadcasted_iota(jnp.int32, (POINTS, POINTS), 1)
    x = (source & (BW - 1)) + ((source >> 7) & 1) * BW
    y = ((source >> 4) & (BH - 1)) + (source >> 8) * BH
    kind = (y & mask) * step + (x & mask)
    place = (y >> log_step) * (2 * BW // step) + (x >> log_step)
    return (kind * (POINTS // (step * step)) + place == lane).astype(jnp.bfloat16)


def sort_rows(picked, nblocks, lanes_at):
    return jnp.concatenate(
        [
            picked[q * nblocks : (q + 1) * nblocks, lanes_at : lanes_at + CELLS]
            for q in range(QUADS)
        ],
        axis=1,
    )


LANES = lax.GatherDimensionNumbers(
    offset_dims=(),
    collapsed_slice_dims=(1,),
    start_index_map=(1,),
    operand_batching_dims=(0,),
    start_indices_batching_dims=(0,),
)


def take_lanes(values, index):
    picked = lax.gather(
        values,
        index[..., None],
        LANES,
        slice_sizes=(1, 1),
        mode=lax.GatherScatterMode.PROMISE_IN_BOUNDS,
    )
    return picked.astype(jnp.float32)


def transport_kernel(
    far_ref,
    regions_ref,
    base_ref,
    order1_ref,
    order2_ref,
    relay,
    mate,
    cross,
    even2,
    odd2,
    mid,
    new_ref,
    displace_ref,
    wind_rows,
    wind_patch,
    rows_ref,
    patch_ref,
    weight_ref,
    layer_ref,
):
    n_tracer, n_level, nblocks, _ = new_ref.shape
    n_comp = displace_ref.shape[0]
    n_ext = n_level + 2
    own = lax.axis_index("tile")
    picks = [
        selectors(regions_ref[k], run_starts(far_ref[k], own), own, nblocks)
        for k in range(ITERS + 1)
    ]
    bands = (odd2, mate, mid, cross, even2, relay)

    def stacked(row):
        return jnp.concatenate([b[row] for b in bands], axis=0)

    n_field = n_comp * n_level
    pick = jnp.concatenate(picks[:ITERS], axis=0)
    for i in range(0, n_field, 2):
        picked = jnp.dot(
            pick,
            jnp.concatenate([stacked(i), stacked(i + 1)], axis=1),
            preferred_element_type=jnp.float32,
        ).astype(jnp.bfloat16)
        for k in range(ITERS):
            part = picked[k * QUADS * nblocks : (k + 1) * QUADS * nblocks]
            for half in range(2):
                at = (k * n_field + i + half) * nblocks
                wind_rows[at : at + nblocks, :] = sort_rows(part, nblocks, half * CELLS)
    wind_patch[...] = jnp.dot(
        wind_rows[...], order1_ref[...], preferred_element_type=jnp.float32
    ).astype(jnp.bfloat16)
    for t in range(n_tracer):
        levels = [stacked(n_field + t * n_level + l) for l in range(n_level)]
        below = stacked(n_field + n_tracer * n_level + t)
        above = stacked(n_field + n_tracer * (n_level + 1) + t)
        levels = [below] + levels + [above]
        for e in range(0, n_ext, 2):
            picked = jnp.dot(
                picks[ITERS],
                jnp.concatenate(levels[e : e + 2], axis=1),
                preferred_element_type=jnp.float32,
            ).astype(jnp.bfloat16)
            for half in range(2):
                at = (t * n_ext + e + half) * nblocks
                rows_ref[at : at + nblocks, :] = sort_rows(picked, nblocks, half * CELLS)
    patch_ref[...] = jnp.dot(
        rows_ref[...], order2_ref[...], preferred_element_type=jnp.float32
    ).astype(jnp.bfloat16)
    displace = [[None] * n_comp for _ in range(n_level)]
    for k in range(ITERS):
        x0 = base_ref[k, 0] + 1
        y0 = base_ref[k, 1] + 1
        xs = [(x0 + 1) >> 1, x0 >> 1]
        ys = [((y0 + 1) >> 1) * BW, (y0 >> 1) * BW]
        index = [[(ys[ry] + xs[rx]).astype(jnp.int16) for rx in range(2)] for ry in range(2)]
        odd_x = (x0 & 1) == 1
        odd_y = (y0 & 1) == 1
        taken = {}
        for ry in range(2):
            for rx in range(2):
                kind = ry * 2 + rx
                for i in range(n_field):
                    at = (k * n_field + i) * nblocks
                    values = wind_patch[at : at + nblocks, kind * 128 : (kind + 1) * 128]
                    taken[i, kind] = take_lanes(values, index[ry][rx])
        for l in range(n_level):
            if k == 0:
                frac_x = jnp.full(x0.shape, 0.5, jnp.float32)
                frac_y = frac_x
            else:
                frac_x = 0.5 + 0.5 * jnp.tanh(displace[l][0])
                frac_y = 0.5 + 0.5 * jnp.tanh(displace[l][1])
            weight_x = [
                jnp.where(odd_x, frac_x, 1.0 - frac_x),
                jnp.where(odd_x, 1.0 - frac_x, frac_x),
            ]
            weight_y = [
                jnp.where(odd_y, frac_y, 1.0 - frac_y),
                jnp.where(odd_y, 1.0 - frac_y, frac_y),
            ]
            for c in range(n_comp):
                total = None
                for ry in range(2):
                    for rx in range(2):
                        term = weight_x[rx] * weight_y[ry] * taken[c * n_level + l, ry * 2 + rx]
                        total = term if total is None else total + term
                displace[l][c] = 0.5 * (mid[c * n_level + l].astype(jnp.float32) + total)
    for l in range(n_level):
        for c in range(n_comp):
            displace_ref[c, l] = displace[l][c]
    x0 = base_ref[ITERS, 0]
    y0 = base_ref[ITERS, 1]
    xs = [((x0 + ((r - x0) & 3)) >> 2) + r * 32 for r in range(4)]
    ys = [((y0 + ((r - y0) & 3)) >> 2) * 8 for r in range(4)]
    index = [(ys[ry] + xs[rx]).astype(jnp.int16) for ry in range(4) for rx in range(4)]
    for l in range(n_level):
        split = []
        for axis, start in ((0, x0), (1, y0)):
            w = lagrange_cubic(1.5 + 0.5 * jnp.tanh(displace[l][axis]))
            bit0 = (start & 1) == 1
            bit1 = (start & 2) == 2
            w = [jnp.where(bit0, w[(r - 1) & 3], w[r]) for r in range(4)]
            w = [jnp.where(bit1, w[(r - 2) & 3], w[r]) for r in range(4)]
            split.append(w)
        for ry in range(4):
            for rx in range(4):
                weight_ref[ry * 4 + rx, l] = split[0][rx] * split[1][ry]
        s = jnp.tanh(displace[l][2])
        layer_ref[l, 0] = 0.5 * s * (s - 1.0)
        layer_ref[l, 1] = 1.0 - s * s
        layer_ref[l, 2] = 0.5 * s * (s + 1.0)

    def one_tracer(t, carry):
        sums = {}
        for kind in range(16):
            at_lane = (kind // 4) * 128
            taken = []
            for e in range(n_ext):
                at = pl.multiple_of((t * n_ext + e) * nblocks, nblocks)
                values = patch_ref[pl.ds(at, nblocks), at_lane : at_lane + 128]
                taken.append(take_lanes(values, index[kind]))
            for l in range(n_level):
                weight = weight_ref[kind, l]
                for d in range(3):
                    term = weight * taken[l + d]
                    sums[l, d] = sums[l, d] + term if kind else term
        for l in range(n_level):
            total = layer_ref[l, 0] * sums[l, 0]
            total = total + layer_ref[l, 1] * sums[l, 1] + layer_ref[l, 2] * sums[l, 2]
            new_ref[t, l] = total.astype(jnp.bfloat16)
        return carry

    lax.fori_loop(0, n_tracer, one_tracer, 0, unroll=4)


def body(tracers, wind_field, regions, stencil_base, far_start):
    n_tracer, n_level, nblocks, cells = tracers.shape
    n_comp = wind_field.shape[0]
    level_pos = lax.axis_index("lev")
    even = level_pos % 2 == 0
    bottom, top = tracers[:, 0], tracers[:, n_level - 1]
    got_odd = swapped(jnp.where(even, bottom, top), "lev", 1, 1)
    got_even = swapped(jnp.where(even, top, bottom), "lev", 0, 1)
    odd = level_pos % 2 == 1
    below = jnp.where(odd, got_even, got_odd)
    above = jnp.where(odd, got_odd, got_even)
    packet = jnp.concatenate(
        [
            wind_field.reshape(-1, nblocks, cells),
            tracers.reshape(-1, nblocks, cells),
            jnp.where(level_pos == 0, bottom, below),
            jnp.where(level_pos == lax.axis_size("lev") - 1, top, above),
        ],
        axis=0,
    )
    odd2 = swapped(packet, "tile", 2, 2)
    even2 = swapped(packet, "tile", 0, 2)
    n_bands = lax.axis_size("tile")
    pairs = [(i, i ^ 3) for i in range(n_bands) if i % 4 in (1, 2)]
    cross = lax.ppermute(packet, "tile", pairs)
    pairs = [(i, i ^ 1) for i in range(2, n_bands - 2) if i % 4 in (1, 2)]
    relay = lax.ppermute(odd2, "tile", pairs)
    mate = swapped(packet, "tile", 0, 1)
    _, zero = lax.optimization_barrier((packet[0, 0], jnp.int32(0)))
    wind_rows = ITERS * n_comp * n_level * nblocks
    rows = n_tracer * (n_level + 2) * nblocks
    vmem = pl.BlockSpec(memory_space=pltpu.VMEM)
    return pl.pallas_call(
        transport_kernel,
        name="transport",
        out_shape=(
            jax.ShapeDtypeStruct(tracers.shape, jnp.bfloat16),
            jax.ShapeDtypeStruct(wind_field.shape, jnp.float32),
        ),
        in_specs=[vmem] * 11,
        out_specs=(vmem, vmem),
        scratch_shapes=[
            pltpu.VMEM((wind_rows, POINTS), jnp.bfloat16),
            pltpu.VMEM((wind_rows, POINTS), jnp.bfloat16),
            pltpu.VMEM((rows, POINTS), jnp.bfloat16),
            pltpu.VMEM((rows, POINTS), jnp.bfloat16),
            pltpu.VMEM((16, n_level, nblocks, cells), jnp.float32),
            pltpu.VMEM((n_level, 3, nblocks, cells), jnp.float32),
        ],
        compiler_params=pltpu.CompilerParams(vmem_limit_bytes=16 * 1024 * 1024),
    )(
        jnp.swapaxes(far_start, 1, 2),
        jnp.swapaxes(regions, 1, 2),
        stencil_base,
        class_order(1, zero),
        class_order(2, zero),
        relay,
        mate,
        cross,
        even2,
        odd2,
        packet,
    )


def solution(mesh):
    return jax.shard_map(
        body,
        mesh=mesh,
        in_specs=(
            P(None, "lev", "tile", None),
            P(None, "lev", "tile", None),
            P(None, "tile", None),
            P(None, None, "tile", None),
            P(),
        ),
        out_specs=(P(None, "lev", "tile", None), P(None, "lev", "tile", None)),
        check_vma=False,
    )
```
